256 devices in a mesh: dp: 4 (over y), expert: 64 (over z, x, core).
Axes of the slice: x: 4, y: 4, z: 8, core: 2. Of those that a mesh axis runs over, the one named last changes fastest.
Arguments:
- tokens: bfloat16 [16384, 2048], P(('dp', 'expert')), may hold values from -6 to 6
- expert_ids: int32 [16384, 6], P(('dp', 'expert')), may hold values from 0 to 63, as said below
- gate_probs: float32 [16384, 6], P(('dp', 'expert')), may hold values from 0.1 to 0.5
- cotangent: bfloat16 [16384, 2048], P(('dp', 'expert')), may hold values from -6 to 6
- gate_proj: bfloat16 [64, 2048, 768], P('expert', 'dp'), may hold values from -0.125 to 0.125
- up_proj: bfloat16 [64, 2048, 768], P('expert', 'dp'), may hold values from -0.125 to 0.125
- down_proj: bfloat16 [64, 2048, 768], P('expert', 'dp'), may hold values from -0.21875 to 0.21875
Outputs:
- mixed: bfloat16 [16384, 2048], P(('dp', 'expert'))
- token_grads: bfloat16 [16384, 2048], P(('dp', 'expert'))
- prob_grads: float32 [16384, 6], P(('dp', 'expert'))
- grad_gate_proj: float32 [64, 2048, 768], P('expert', 'dp')
- grad_up_proj: float32 [64, 2048, 768], P('expert', 'dp')
- grad_down_proj: float32 [64, 2048, 768], P('expert', 'dp')
The draws below stay inside these ranges and needn't reach their ends.
Inputs may be any that keep to these rules, and one draw needn't show every extreme that they name: `expert_ids`: each row names 6 different experts. Among the 64 rows of one device no expert is named by more than 8 rows, and in every data group some expert is named by exactly 8 rows of every device of that group.
All inputs are finite; a program needn't handle non-finite values.
Results may differ from the reference program's by a relative error of at most 0.0065.
Values may be sent and summed in bfloat16 or wider, within the bound.
A program may use at most 128 MiB of HBM per device.

```python
import jax
import jax.numpy as jnp
from jax import lax

D = 2048
TOPK = 6
FF = 768
TOK_DEV = 64
EXPERTS = 64
CAP = 8
TOKENS = 16384


def shuffle_order(sub_key):
    return jax.random.permutation(sub_key, TOK_DEV)


def draw_expert_ids(key, part):
    blocks = TOKENS // TOK_DEV
    group_count = blocks // EXPERTS
    candidates = EXPERTS * CAP
    levels = jax.random.randint(jax.random.fold_in(key, 11), (group_count, EXPERTS), 0, 4)
    favoured = jax.random.randint(jax.random.fold_in(key, 12), (group_count,), 0, EXPERTS)
    levels = jnp.where(jnp.arange(EXPERTS, dtype=jnp.int32)[None, :] == favoured[:, None], 8, levels)
    block_group = jnp.arange(blocks, dtype=jnp.int32) // EXPERTS
    block_levels = jnp.take(levels, block_group, axis=0)
    jitter = jax.random.randint(jax.random.fold_in(key, 13), (blocks, EXPERTS, CAP), 0, 4096)
    serial = jnp.arange(candidates, dtype=jnp.int32).reshape(EXPERTS, CAP)
    scores = ((block_levels[:, :, None] * 4096 + jitter) * candidates + serial[None, :, :]).reshape(blocks, candidates)
    unused, chosen = lax.top_k(scores, TOK_DEV * TOPK)
    chosen = jnp.sort(chosen, axis=1)
    table = (chosen // CAP).reshape(blocks, TOPK, TOK_DEV)
    table = jnp.transpose(table, (0, 2, 1))
    perm_keys = jax.random.split(jax.random.fold_in(key, 14), blocks)
    orders = jax.vmap(shuffle_order)(perm_keys)
    table = jnp.take_along_axis(table, orders[:, :, None], axis=1)
    shifts = jax.random.randint(jax.random.fold_in(key, 15), (blocks, TOK_DEV, 1), 0, TOPK)
    rotate = (jnp.arange(TOPK, dtype=jnp.int32)[None, None, :] + shifts) % TOPK
    table = jnp.take_along_axis(table, rotate, axis=2)
    return table.reshape(TOKENS, TOPK).astype(jnp.int32)


def steps_of(key, extent, shards, smallest, largest):
    def one(dim, shards_of):
        steps = jax.random.uniform(jax.random.fold_in(jax.random.fold_in(key, 6), dim), (shards_of,), jnp.float32, smallest / len(shards), largest / len(shards))
        return jnp.repeat(jnp.exp(steps), extent[dim] // shards_of).reshape((-1,) + (1,) * (len(extent) - dim - 1))

    loudness = one(*shards[0])
    for cut in shards[1:]:
        loudness = loudness * one(*cut)
    return loudness


def bell_draw(stream_key, extent, deviation, reach, shards=(), kind=jnp.bfloat16):
    gain = steps_of(stream_key, extent, shards, -0.22, 0.18) if shards else 1.0
    array = jax.random.normal(stream_key, extent, jnp.float32) * deviation * gain
    return jnp.minimum(jnp.maximum(array, -reach), reach).astype(kind)


def setup_inputs(seed: int = 0) -> dict:
    arg_keys = jax.random.split(jax.random.key(seed), 8)
    tokens = bell_draw(arg_keys[0], (TOKENS, D), 1.0, 6.0, ((0, 256),))
    expert_ids = draw_expert_ids(jax.random.fold_in(arg_keys[7], 71), 0)
    gate_probs = jnp.clip(0.1 + 0.4 * jax.random.uniform(arg_keys[2], (TOKENS, TOPK), jnp.float32) ** steps_of(arg_keys[2], (TOKENS, TOPK), ((0, 256),), -0.2, 0.2), 0.1, 0.5)
    cotangent = bell_draw(arg_keys[3], (TOKENS, D), 1.0, 6.0, ((0, 256),))
    gate_proj = bell_draw(arg_keys[4], (EXPERTS, D, FF), D ** -0.5, 0.125, ((0, 64), (1, 4)))
    up_proj = bell_draw(arg_keys[5], (EXPERTS, D, FF), D ** -0.5, 0.125, ((0, 64), (1, 4)))
    down_proj = bell_draw(arg_keys[6], (EXPERTS, D, FF), FF ** -0.5, 0.21875, ((0, 64), (1, 4)))
    return {"tokens": tokens, "expert_ids": expert_ids, "gate_probs": gate_probs, "cotangent": cotangent, "gate_proj": gate_proj, "up_proj": up_proj, "down_proj": down_proj}


def routing_slots(expert_ids):
    onehot = (expert_ids[:, :, None] == jnp.arange(EXPERTS, dtype=jnp.int32)[None, None, :]).astype(jnp.int32)
    per_token = jnp.sum(onehot, axis=1)
    earlier = jnp.cumsum(per_token, axis=0) - per_token
    return jnp.sum(onehot * earlier[:, None, :], axis=2).astype(jnp.int32)


def forward_rows(rows, gate_proj, up_proj, down_proj):
    gate_pre = jnp.dot(rows, gate_proj, preferred_element_type=jnp.float32)
    up_pre = jnp.dot(rows, up_proj, preferred_element_type=jnp.float32)
    hidden = (jax.nn.silu(gate_pre) * up_pre).astype(jnp.bfloat16)
    expert_out = lax.dot_general(hidden, down_proj, (((1,), (1,)), ((), ())), preferred_element_type=jnp.float32).astype(jnp.bfloat16)
    return expert_out, gate_pre, up_pre, hidden


def backward_rows(grad_rows, gate_pre, up_pre, gate_proj, up_proj, down_proj):
    d_hidden = jnp.dot(grad_rows, down_proj, preferred_element_type=jnp.float32)
    sigmoid_gate = jax.nn.sigmoid(gate_pre)
    silu_gate = gate_pre * sigmoid_gate
    d_gate = (d_hidden * up_pre * sigmoid_gate * (1.0 + gate_pre * (1.0 - sigmoid_gate))).astype(jnp.bfloat16)
    d_up = (d_hidden * silu_gate).astype(jnp.bfloat16)
    across = (((1,), (1,)), ((), ()))
    d_rows = lax.dot_general(d_gate, gate_proj, across, preferred_element_type=jnp.float32)
    d_rows = d_rows + lax.dot_general(d_up, up_proj, across, preferred_element_type=jnp.float32)
    return d_rows.astype(jnp.bfloat16), d_gate, d_up


def place_rows(spots, rows):
    empty = jnp.zeros((EXPERTS * CAP, D), rows.dtype)
    return empty.at[spots.reshape(-1)].set(rows.reshape(-1, D))


def pick_rows(source_rows, spots):
    return jnp.take(source_rows, spots.reshape(-1), axis=0)


def reference(tokens, expert_ids, gate_probs, cotangent, gate_proj, up_proj, down_proj):
    blocks = TOKENS // TOK_DEV
    ids_block = expert_ids.reshape(blocks, TOK_DEV, TOPK)
    slot_index = jax.vmap(routing_slots)(ids_block)
    position = (ids_block * CAP + slot_index).astype(jnp.int32)
    token_rows = jnp.broadcast_to(tokens.reshape(blocks, TOK_DEV, 1, D), (blocks, TOK_DEV, TOPK, D))
    scaled = (gate_probs.reshape(blocks, TOK_DEV, TOPK, 1) * cotangent.reshape(blocks, TOK_DEV, 1, D).astype(jnp.float32)).astype(jnp.bfloat16)
    slot_rows = jax.vmap(place_rows)(position, token_rows).reshape(blocks, EXPERTS, CAP, D)
    slot_grads = jax.vmap(place_rows)(position, scaled).reshape(blocks, EXPERTS, CAP, D)
    contract_rows = (((0,), (0,)), ((), ()))

    def one_expert(expert_id):
        rows_in = lax.dynamic_index_in_dim(slot_rows, expert_id, 1, keepdims=False).reshape(blocks * CAP, D)
        grads_in = lax.dynamic_index_in_dim(slot_grads, expert_id, 1, keepdims=False).reshape(blocks * CAP, D)
        gate_one = lax.dynamic_index_in_dim(gate_proj, expert_id, 0, keepdims=False)
        up_one = lax.dynamic_index_in_dim(up_proj, expert_id, 0, keepdims=False)
        down_one = lax.dynamic_index_in_dim(down_proj, expert_id, 0, keepdims=False)
        expert_out, gate_pre, up_pre, hidden = forward_rows(rows_in, gate_one, up_one, down_one)
        d_rows, d_gate, d_up = backward_rows(grads_in, gate_pre, up_pre, gate_one, up_one, down_one)
        grad_gate = lax.dot_general(rows_in, d_gate, contract_rows, preferred_element_type=jnp.float32)
        grad_up = lax.dot_general(rows_in, d_up, contract_rows, preferred_element_type=jnp.float32)
        grad_down = lax.dot_general(grads_in, hidden, contract_rows, preferred_element_type=jnp.float32)
        return expert_out.reshape(blocks, CAP, D), d_rows.reshape(blocks, CAP, D), grad_gate, grad_up, grad_down

    outs_all, rows_all, grad_gate, grad_up, grad_down = lax.map(one_expert, jnp.arange(EXPERTS, dtype=jnp.int32))
    returned = jnp.transpose(outs_all, (1, 0, 2, 3)).reshape(blocks, EXPERTS * CAP, D)
    grad_back = jnp.transpose(rows_all, (1, 0, 2, 3)).reshape(blocks, EXPERTS * CAP, D)
    picked = jax.vmap(pick_rows)(returned, position).reshape(blocks, TOK_DEV, TOPK, D).astype(jnp.float32)
    picked_grads = jax.vmap(pick_rows)(grad_back, position).reshape(blocks, TOK_DEV, TOPK, D).astype(jnp.float32)
    mixed = jnp.sum(gate_probs.reshape(blocks, TOK_DEV, TOPK, 1) * picked, axis=2).astype(jnp.bfloat16).reshape(TOKENS, D)
    prob_grads = jnp.sum(cotangent.reshape(blocks, TOK_DEV, 1, D).astype(jnp.float32) * picked, axis=3).reshape(TOKENS, TOPK)
    token_grads = jnp.sum(picked_grads, axis=2).astype(jnp.bfloat16).reshape(TOKENS, D)
    return (mixed, token_grads, prob_grads, grad_gate, grad_up, grad_down)
```

```python
import jax
import jax.numpy as jnp
from jax import lax
from jax.sharding import PartitionSpec as P


def routing_slots(expert_ids, experts):
    onehot = (expert_ids[:, :, None] == jnp.arange(experts, dtype=jnp.int32)[None, None, :]).astype(
        jnp.int32
    )
    per_token = jnp.sum(onehot, axis=1)
    earlier = jnp.cumsum(per_token, axis=0) - per_token
    return jnp.sum(onehot * earlier[:, None, :], axis=2)


def forward_rows(rows, gate_proj, up_proj, down_proj):
    gate_pre = jnp.dot(rows, gate_proj, preferred_element_type=jnp.float32)
    up_pre = jnp.dot(rows, up_proj, preferred_element_type=jnp.float32)
    hidden = (jax.nn.silu(gate_pre) * up_pre).astype(jnp.bfloat16)
    expert_out = lax.dot_general(
        hidden, down_proj, (((1,), (1,)), ((), ())), preferred_element_type=jnp.float32
    ).astype(jnp.bfloat16)
    return (expert_out, gate_pre, up_pre, hidden)


def backward_rows(grad_rows, gate_pre, up_pre, gate_proj, up_proj, down_proj):
    d_hidden = jnp.dot(grad_rows, down_proj, preferred_element_type=jnp.float32)
    sigmoid_gate = jax.nn.sigmoid(gate_pre)
    silu_gate = gate_pre * sigmoid_gate
    d_gate = (d_hidden * up_pre * sigmoid_gate * (1.0 + gate_pre * (1.0 - sigmoid_gate))).astype(
        jnp.bfloat16
    )
    d_up = (d_hidden * silu_gate).astype(jnp.bfloat16)
    across = (((1,), (1,)), ((), ()))
    d_rows = lax.dot_general(d_gate, gate_proj, across, preferred_element_type=jnp.float32)
    d_rows = d_rows + lax.dot_general(d_up, up_proj, across, preferred_element_type=jnp.float32)
    return (d_rows.astype(jnp.bfloat16), d_gate, d_up)


def pick_rows(source_rows, position, top_count):
    chosen = jnp.take(source_rows, position.reshape(-1), axis=0)
    return chosen.reshape(position.shape[0], top_count, source_rows.shape[1])


def on_device(tokens, expert_ids, gate_probs, cotangent, gate_proj, up_proj, down_proj):
    experts = lax.axis_size("expert")
    tok_dev, top_count = expert_ids.shape
    model_width = tokens.shape[1]
    capacity = min(tok_dev, (tok_dev * top_count * 4 + 3 * experts - 1) // (3 * experts))
    slot_index = routing_slots(expert_ids, experts)
    position = expert_ids * capacity + slot_index
    placing = (
        position[None, :, :] == jnp.arange(experts * capacity, dtype=jnp.int32)[:, None, None]
    ).astype(jnp.float32)
    placer = jnp.sum(placing, axis=2)
    weighted = jnp.sum(placing * gate_probs[None, :, :], axis=2)
    row_send = (
        jnp.dot(placer.astype(jnp.bfloat16), tokens, preferred_element_type=jnp.float32)
        .astype(jnp.bfloat16)
        .reshape(experts, capacity, model_width)
    )
    grad_send = (
        jnp.dot(weighted, cotangent.astype(jnp.float32), precision=lax.Precision.HIGHEST)
        .astype(jnp.bfloat16)
        .reshape(experts, capacity, model_width)
    )
    both = lax.all_gather(
        jnp.concatenate([gate_proj[0], up_proj[0]], axis=1), "dp", axis=0, tiled=True
    )
    full_gate, full_up = both[:, : gate_proj.shape[2]], both[:, gate_proj.shape[2] :]
    full_down = lax.all_gather(down_proj[0], "dp", axis=0, tiled=True)
    rows_in = lax.all_to_all(row_send, "expert", split_axis=0, concat_axis=0, tiled=True)
    rows_flat = rows_in.reshape(-1, model_width)
    expert_out, gate_pre, up_pre, hidden = forward_rows(rows_flat, full_gate, full_up, full_down)
    returned = lax.all_to_all(
        expert_out.reshape(experts, capacity, model_width),
        "expert",
        split_axis=0,
        concat_axis=0,
        tiled=True,
    )
    grads_in = lax.all_to_all(grad_send, "expert", split_axis=0, concat_axis=0, tiled=True)
    grads_flat = grads_in.reshape(-1, model_width)
    d_rows, d_gate, d_up = backward_rows(
        grads_flat, gate_pre, up_pre, full_gate, full_up, full_down
    )
    grad_back = lax.all_to_all(
        d_rows.reshape(experts, capacity, model_width),
        "expert",
        split_axis=0,
        concat_axis=0,
        tiled=True,
    )
    picked = pick_rows(returned.reshape(-1, model_width), position, top_count).astype(jnp.float32)
    mixed = jnp.sum(gate_probs[:, :, None] * picked, axis=1).astype(jnp.bfloat16)
    prob_grads = jnp.sum(cotangent.astype(jnp.float32)[:, None, :] * picked, axis=2)
    picked_grads = pick_rows(grad_back.reshape(-1, model_width), position, top_count).astype(
        jnp.float32
    )
    token_grads = jnp.sum(picked_grads, axis=1).astype(jnp.bfloat16)
    contract_rows = (((0,), (0,)), ((), ()))
    hidden_units = hidden.shape[1]
    gate_term = lax.dot_general(
        rows_flat, d_gate, contract_rows, preferred_element_type=jnp.float32
    )
    up_term = lax.dot_general(rows_flat, d_up, contract_rows, preferred_element_type=jnp.float32)
    down_term = lax.dot_general(
        grads_flat, hidden, contract_rows, preferred_element_type=jnp.float32
    )
    grad_down = lax.psum_scatter(
        down_term.astype(jnp.bfloat16), "dp", scatter_dimension=0, tiled=True
    ).astype(jnp.float32)
    shares = lax.psum_scatter(
        jnp.concatenate([gate_term, up_term], axis=1).astype(jnp.bfloat16),
        "dp",
        scatter_dimension=0,
        tiled=True,
    ).astype(jnp.float32)
    grad_gate = shares[:, :hidden_units]
    grad_up = shares[:, hidden_units:]
    return (mixed, token_grads, prob_grads, grad_gate[None], grad_up[None], grad_down[None])


def solution(mesh):
    in_specs = (
        P(("dp", "expert"), None),
        P(("dp", "expert"), None),
        P(("dp", "expert"), None),
        P(("dp", "expert"), None),
        P("expert", "dp", None),
        P("expert", "dp", None),
        P("expert", "dp", None),
    )
    out_specs = (
        P(("dp", "expert"), None),
        P(("dp", "expert"), None),
        P(("dp", "expert"), None),
        P("expert", "dp", None),
        P("expert", "dp", None),
        P("expert", "dp", None),
    )
    return jax.shard_map(
        on_device, mesh=mesh, in_specs=in_specs, out_specs=out_specs, check_vma=False
    )
```

```python
import jax
import jax.numpy as jnp
from jax import lax
from jax.experimental import pallas as pl
from jax.experimental.pallas import tpu as pltpu
from jax.sharding import PartitionSpec as P

MESH = pl.DeviceIdType.MESH
BF = jnp.bfloat16
F32 = jnp.float32
NY, NZ, NX, NC = 4, 8, 4, 2
TOK, D, FF, CAP, TOPK = 64, 2048, 768, 8, 6
ROWS = NX * NC * NZ * CAP
GR = 2 * TOK
DY = D // NY
HALF = DY // 2
NT = (((1,), (1,)), ((), ()))
TN = (((0,), (0,)), ((), ()))


def dot(a, b, dims=(((1,), (0,)), ((), ()))):
    return lax.dot_general(a, b, dims, preferred_element_type=F32)


def kernel(
    tok, cot, meta, gw, uw, dw,
    mixed_o, tgrad_o, pg_o, og, ou, od,
    zt, zc, zm, xs_r, xs_g, rows, grads, gu, dn, gp, hid, dgu, xr_o, xr_d,
    pm, wm, zs_o, zr_o, zs_d, zr_d, pgs, pgr, acc_o, acc_d,
    d1, d2, d3, dhp, dhm, dfp, dfm, down,
    g1, g2, g3, ghp, ghm, gfp, gfm, gown,
    ssem, rsem, lsem,
):
    y = lax.axis_index("dp")
    e = lax.axis_index("expert")
    z, x, c = e // (NX * NC), (e // NC) % NX, e % NC

    def at(dy=0, dz=0, dx=0, dc=0):
        return (
            (y + dy + NY) % NY,
            ((z + dz + NZ) % NZ) * (NX * NC) + ((x + dx + NX) % NX) * NC + (c + dc) % NC,
        )

    yp, ym, zp, zq = at(dy=1), at(dy=-1), at(dz=1), at(dz=-1)
    offsets = [(k // NC, k % NC) for k in range(NX * NC)]
    to_x = [at(dx=dx, dc=dc) for dx, dc in offsets]
    from_x = [at(dx=-dx, dc=dc) for dx, dc in offsets]

    barrier = pltpu.get_barrier_semaphore()
    peers = [yp, ym, zp, zq] + to_x[1:]
    for peer in peers:
        pl.semaphore_signal(barrier, inc=1, device_id=peer, device_id_type=MESH)
    pl.semaphore_wait(barrier, len(peers))

    used = [0, 0]
    started = []

    def send(src, dst, peer):
        i = used[0]
        used[0] += 1
        copy = pltpu.make_async_remote_copy(
            src_ref=src, dst_ref=dst, send_sem=ssem.at[i], recv_sem=rsem.at[i],
            device_id=peer, device_id_type=MESH,
        )
        copy.start()
        started.append(copy)
        return copy

    def local(src, dst):
        i = used[1]
        used[1] += 1
        copy = pltpu.make_async_copy(src, dst, lsem.at[i])
        copy.start()
        return copy

    def yrows(dy, start=0, size=DY):
        return pl.ds(pl.multiple_of(((y + dy + NY) % NY) * DY + start, HALF), size)

    gcol, ucol = pl.ds(0, FF), pl.ds(FF, FF)

    def own(w, full, cols):
        dst = full.at[yrows(0), cols]
        return send(w, dst, yp), send(w, dst, ym)

    def relay(pair, full, cols):
        pair[0].wait_recv()
        a = full.at[yrows(-1, 0, HALF), cols]
        first = send(a, a, yp)
        pair[1].wait_recv()
        b = full.at[yrows(1, HALF, HALF), cols]
        return first, send(b, b, ym)

    gate_own = own(gw, gu, gcol)
    up_own = own(uw, gu, ucol)

    def zblock(buf, j, zi, start=0, size=TOK):
        return buf.at[pl.ds(j * GR + zi * TOK + start, size), :]

    def zstep(buf, src, s):
        if s == 0:
            return send(src, zblock(buf, 0, 0), zp), send(src, zblock(buf, 0, 1), zq)
        if s < 3:
            return (
                send(zblock(buf, s - 1, 0), zblock(buf, s, 0), zp),
                send(zblock(buf, s - 1, 1), zblock(buf, s, 1), zq),
            )
        h = TOK // 2
        return (
            send(zblock(buf, 2, 0, 0, h), zblock(buf, 3, 1, 0, h), zp),
            send(zblock(buf, 2, 1, h, h), zblock(buf, 3, 1, h, h), zq),
        )

    def mstep(s):
        if s == 0:
            return send(meta, zm.at[0, 0], zp), send(meta, zm.at[0, 1], zq)
        if s < 3:
            return send(zm.at[s - 1, 0], zm.at[s, 0], zp), send(zm.at[s - 1, 1], zm.at[s, 1], zq)
        return (send(zm.at[2, 0], zm.at[3, 1], zp),)

    m_now = mstep(0)
    t_now = zstep(zt, tok, 0)
    loads = [
        local(gw, gu.at[yrows(0), gcol]),
        local(uw, gu.at[yrows(0), ucol]),
        local(dw, dn.at[yrows(0), :]),
        local(tok, zblock(zt, 3, 0)),
        local(cot, zblock(zc, 3, 0)),
    ]
    zm[3, 0] = meta[...]

    row = lax.broadcasted_iota(jnp.int32, (GR, GR), 0)
    lane = lax.broadcasted_iota(jnp.int32, (GR, GR), 1)
    kk = row >> 4
    expert = (z * (NX * NC) + (((x + (kk >> 1)) & (NX - 1)) << 1) + ((c + kk) & 1)).astype(F32)
    slot = (row & (CAP - 1)).astype(F32)
    same_block = ((row >> 3) & 1) == (lane >> 6)
    earlier = jnp.where(((row >> 6) == (lane >> 6)) & (row < lane), 1.0, 0.0).astype(BF)
    low = lax.broadcasted_iota(jnp.int32, (16, GR), 1) < TOK

    def joined(j):
        return jnp.where(low, zm[j, 0], zm[j, 1])

    def route(j):
        both = joined(j)
        named = jnp.zeros((GR, GR), F32)
        weight = jnp.zeros((GR, GR), F32)
        for i in range(TOPK):
            hit = both[i : i + 1, :] == expert
            named = jnp.where(hit, 1.0, named)
            weight = weight + jnp.where(hit, both[8 + i : 9 + i, :], 0.0)
        rank = dot(named.astype(BF), earlier)
        fits = (named > 0.5) & (rank == slot) & same_block
        pm[j] = jnp.where(fits, 1.0, 0.0).astype(BF)
        wm[j] = jnp.where(fits, weight, 0.0)

    def group(buf, j):
        return buf.at[pl.ds(j * GR, GR), :]

    def piece(buf, j, k):
        return buf.at[pl.ds(j * GR + k * 16, 16), :]

    def xsend(src, dst, j, targets):
        return [send(piece(src, j, k), piece(dst, j, k), targets[k]) for k in range(1, NX * NC)]

    dispatched = []

    def dispatch_rows(j):
        filled = dot(pm[j], group(zt, j)[...]).astype(BF)
        group(xs_r, j)[...] = filled
        piece(rows, j, 0)[...] = filled[:16]
        dispatched.extend(xsend(xs_r, rows, j, to_x))

    def dispatch_grads(j):
        prob = jnp.sum(wm[j], axis=1, keepdims=True)
        filled = (dot(pm[j], group(zc, j)[...]) * prob).astype(BF)
        group(xs_g, j)[...] = filled
        piece(grads, j, 0)[...] = filled[:16]
        dispatched.extend(xsend(xs_g, grads, j, to_x))

    c_now = None
    gate_far = up_far = down_own = None
    for s in range(1, 5):
        t_next = m_next = None
        for copy in m_now:
            copy.wait_recv()
        if s < 4:
            m_now = mstep(s)
        for copy in t_now:
            copy.wait_recv()
        if s < 4:
            t_now = zstep(zt, tok, s)
        if s == 3:
            gate_far = relay(gate_own, gu, gcol)
        if s == 3:
            c_now = zstep(zc, cot, 0)
        if s == 4:
            loads[3].wait()
        route(s - 1)
        dispatch_rows(s - 1)
    loads[4].wait()
    for s in range(1, 5):
        for copy in c_now:
            copy.wait_recv()
        if s < 4:
            c_now = zstep(zc, cot, s)
        if s == 3:
            up_far = relay(up_own, gu, ucol)
            down_own = own(dw, dn, slice(None))
        dispatch_grads(s - 1)

    for copy in loads[:3]:
        copy.wait()
    for copy in dispatched[: 4 * 7]:
        copy.wait_recv()
    for copy in gate_far + up_far:
        copy.wait_recv()

    def forward_tile(n, carry):
        a = pl.ds(pl.multiple_of(n * 256, 256), 256)
        b = pl.ds(pl.multiple_of(n * 256 + FF, 256), 256)
        gate_pre = dot(rows[...], gu[:, a])
        gp[:, a] = gate_pre
        up_pre = dot(rows[...], gu[:, b])
        gp[:, b] = up_pre
        hid[:, a] = (gate_pre * (1.0 / (1.0 + jnp.exp(-gate_pre))) * up_pre).astype(BF)
        return carry

    lax.fori_loop(0, FF // 256, forward_tile, 0)
    for copy in dispatched[4 * 7 :]:
        copy.wait_recv()

    def term(src, rhs, dy, store):
        def tile(i, carry):
            cols = pl.ds(pl.multiple_of(((y + dy + NY) % NY) * DY + i * 256, 256), 256)
            store(pl.ds(pl.multiple_of(i * 256, 256), 256), dot(src[:, cols], rhs[...], TN))
            return carry

        lax.fori_loop(0, DY // 256, tile, 0)

    def into(buf):
        def store(where, value):
            buf[where, :] = value.astype(buf.dtype)

        return store

    lo, hi = pl.ds(0, HALF), pl.ds(HALF, HALF)

    def shares(src, rhs, s1, s2, s3, hp, hm, fp, fm, mine):
        term(src, rhs, 2, into(s2))
        half_p = send(s2.at[lo, :], hp, yp)
        half_m = send(s2.at[hi, :], hm, ym)
        term(src, rhs, 1, into(s1))
        last = [send(s1.at[hi, :], fp.at[hi, :], yp)]
        term(src, rhs, -1, into(s3))
        last.append(send(s3.at[lo, :], fm.at[lo, :], ym))
        term(src, rhs, 0, into(mine))
        return half_p, half_m, last

    def pass_on(state, s1, s3, hp, hm, fp, fm):
        half_p, half_m, last = state
        half_p.wait_recv()

        def add_p(i, carry):
            r = pl.ds(pl.multiple_of(i * 64, 64), 64)
            s1[r, :] = (s1[r, :].astype(F32) + hp[r, :].astype(F32)).astype(BF)
            return carry

        lax.fori_loop(0, HALF // 64, add_p, 0)
        last.append(send(s1.at[lo, :], fp.at[lo, :], yp))
        half_m.wait_recv()

        def add_m(i, carry):
            r = pl.ds(pl.multiple_of(i * 64, 64), 64)
            t = pl.ds(pl.multiple_of(i * 64 + HALF, 64), 64)
            s3[t, :] = (s3[t, :].astype(F32) + hm[r, :].astype(F32)).astype(BF)
            return carry

        lax.fori_loop(0, HALF // 64, add_m, 0)
        last.append(send(s3.at[hi, :], fm.at[hi, :], ym))
        return last

    def finish(last, mine, fp, fm):
        for copy in last:
            copy.wait_recv()

        def add(i, carry):
            r = pl.ds(pl.multiple_of(i * 64, 64), 64)
            mine[r, :] = mine[r, :] + fp[r, :].astype(F32) + fm[r, :].astype(F32)
            return carry

        lax.fori_loop(0, DY // 64, add, 0)

    down_far = relay(down_own, dn, slice(None))
    down_state = shares(grads, hid, d1, d2, d3, dhp, dhm, dfp, dfm, down)
    for copy in down_far:
        copy.wait_recv()
    for copy in dispatched:
        copy.wait_send()

    def out_tile(n, carry):
        a = pl.ds(pl.multiple_of(n * 256, 256), 256)
        xs_r[:, a] = dot(hid[...], dn[a, :], NT).astype(BF)
        return carry

    lax.fori_loop(0, D // 256, out_tile, 0)
    back_o = {}
    for j in (3, 2, 1, 0):
        back_o[j] = xsend(xs_r, xr_o, j, from_x)
        piece(xr_o, j, 0)[...] = piece(xs_r, j, 0)[...]

    def backward_tile(n, carry):
        a = pl.ds(pl.multiple_of(n * 256, 256), 256)
        b = pl.ds(pl.multiple_of(n * 256 + FF, 256), 256)
        d_hidden = dot(grads[...], dn[:, a])
        gate_pre = gp[:, a]
        q = 1.0 / (1.0 + jnp.exp(-gate_pre))
        dgu[:, a] = (d_hidden * gp[:, b] * q * (1.0 + gate_pre * (1.0 - q))).astype(BF)
        dgu[:, b] = (d_hidden * (gate_pre * q)).astype(BF)
        return carry

    lax.fori_loop(0, FF // 256, backward_tile, 0)
    down_last = pass_on(down_state, d1, d3, dhp, dhm, dfp, dfm)
    gu_state = shares(rows, dgu, g1, g2, g3, ghp, ghm, gfp, gfm, gown)

    def d_rows_tile(n, carry):
        a = pl.ds(pl.multiple_of(n * 256, 256), 256)
        xs_g[:, a] = dot(dgu[...], gu[a, :], NT).astype(BF)
        return carry

    lax.fori_loop(0, D // 256, d_rows_tile, 0)
    back_d = {}
    for j in (3, 2, 1, 0):
        back_d[j] = xsend(xs_g, xr_d, j, from_x)
        piece(xr_d, j, 0)[...] = piece(xs_g, j, 0)[...]

    def ring(q, part, zs, zr, acc, prev):
        h = TOK // 2
        if q == 0:
            acc[...] = part[:TOK]
            zs[0, 0, :h] = part[TOK : TOK + h].astype(BF)
            zs[1, 0, :h] = part[TOK + h :].astype(BF)
            return (
                send(zs.at[0, 0, pl.ds(0, h)], zr.at[0, 0, pl.ds(0, h)], zp),
                send(zs.at[1, 0, pl.ds(0, h)], zr.at[1, 0, pl.ds(0, h)], zq),
            )
        p0, p1 = part[:TOK], part[TOK:]
        prev[0].wait_recv()
        if q == 1:
            zs[0, q, :h] = (p1[:h] + zr[0, 0, :h].astype(F32)).astype(BF)
            zs[0, q, h:] = p1[h:].astype(BF)
        else:
            zs[0, q] = (p1 + zr[0, q - 1].astype(F32)).astype(BF)
        first = send(zs.at[0, q], zr.at[0, q], zp)
        prev[1].wait_recv()
        if q == 1:
            zs[1, q, h:] = (p0[h:] + zr[1, 0, :h].astype(F32)).astype(BF)
            zs[1, q, :h] = p0[:h].astype(BF)
        else:
            zs[1, q] = (p0 + zr[1, q - 1].astype(F32)).astype(BF)
        return first, send(zs.at[1, q], zr.at[1, q], zq)

    def ring_small(q, part, prev):
        if q == 0:
            pgs[1, 0] = part
            pgs[0, 0] = part
            return (send(pgs.at[0, 0], pgr.at[0, 0], zp),)
        prev[0].wait_recv()
        pgs[0, q] = part + pgr[0, q - 1]
        first = send(pgs.at[0, q], pgr.at[0, q], zp)
        if q == 1:
            pgs[1, q] = part
        else:
            prev[1].wait_recv()
            pgs[1, q] = part + pgr[1, q - 1]
        return first, send(pgs.at[1, q], pgr.at[1, q], zq)

    ring_o = ring_p = ring_d = None
    for q in range(4):
        j = 3 - q
        for copy in back_o[j]:
            copy.wait_recv()
        returned = group(xr_o, j)[...]
        w = wm[j]
        w_hi = w.astype(BF)
        w_lo = (w - w_hi.astype(F32)).astype(BF)
        part = dot(w_hi, returned, TN) + dot(w_lo, returned, TN)
        ring_o = ring(q, part, zs_o, zr_o, acc_o, ring_o)
        scores = dot(returned, group(zc, j)[...], NT) * pm[j].astype(F32)
        both = joined(j)
        small = [
            jnp.sum(jnp.where(both[i : i + 1, :] == expert, scores, 0.0), axis=0, keepdims=True)
            for i in range(TOPK)
        ]
        small = jnp.concatenate(small + [jnp.zeros((2, GR), F32)], axis=0)
        ring_p = ring_small(q, small, ring_p)
    gu_last = pass_on(gu_state, g1, g3, ghp, ghm, gfp, gfm)
    for q in range(4):
        j = 3 - q
        for copy in back_d[j]:
            copy.wait_recv()
        part = dot(pm[j], group(xr_d, j)[...], TN)
        ring_d = ring(q, part, zs_d, zr_d, acc_d, ring_d)

    for copy in ring_o + ring_p:
        copy.wait_recv()
    mixed_o[...] = (acc_o[...] + zr_o[0, 3].astype(F32) + zr_o[1, 3].astype(F32)).astype(BF)
    pg_o[...] = pgs[1, 0] + pgr[1, 3] + pltpu.roll(pgr[0, 3], TOK, 1)
    finish(down_last, down, dfp, dfm)
    stores = [local(down, od)]
    for copy in ring_d:
        copy.wait_recv()
    tgrad_o[...] = (acc_d[...] + zr_d[0, 3].astype(F32) + zr_d[1, 3].astype(F32)).astype(BF)
    finish(gu_last, gown, gfp, gfm)
    stores.append(local(gown.at[:, gcol], og))
    stores.append(local(gown.at[:, ucol], ou))
    for copy in started:
        if not any(copy is other for other in dispatched):
            copy.wait_send()
    for copy in stores:
        copy.wait()


def layer(tokens, expert_ids, gate_probs, cotangent, gate_proj, up_proj, down_proj):
    ids = jnp.pad(expert_ids.T.astype(F32), ((0, 8 - TOPK), (0, 0)), constant_values=-1.0)
    probs = jnp.pad(gate_probs.T, ((0, 8 - TOPK), (0, 0)))
    meta = jnp.tile(jnp.concatenate([ids, probs], axis=0), (1, 2))
    vmem = pl.BlockSpec(memory_space=pltpu.VMEM)
    anywhere = pl.BlockSpec(memory_space=pl.ANY)
    v = pltpu.VMEM
    block = [v((DY, FF), BF)] * 3 + [v((HALF, FF), BF)] * 2 + [v((DY, FF), BF)] * 2
    wide = [v((DY, 2 * FF), BF)] * 3 + [v((HALF, 2 * FF), BF)] * 2 + [v((DY, 2 * FF), BF)] * 2
    scratch = [
        v((4 * GR, D), BF), v((4 * GR, D), BF), v((4, 2, 16, GR), F32),
        v((ROWS, D), BF), v((ROWS, D), BF), v((ROWS, D), BF), v((ROWS, D), BF),
        v((D, 2 * FF), BF), v((D, FF), BF),
        v((ROWS, 2 * FF), F32), v((ROWS, FF), BF), v((ROWS, 2 * FF), BF),
        v((ROWS, D), BF), v((ROWS, D), BF),
        v((4, GR, GR), BF), v((4, GR, GR), F32),
        v((2, 4, TOK, D), BF), v((2, 4, TOK, D), BF), v((2, 4, TOK, D), BF), v((2, 4, TOK, D), BF),
        v((2, 4, 8, GR), F32), v((2, 4, 8, GR), F32), v((TOK, D), F32), v((TOK, D), F32),
        *block, v((DY, FF), F32), *wide, v((DY, 2 * FF), F32),
        pltpu.SemaphoreType.DMA((192,)), pltpu.SemaphoreType.DMA((192,)), pltpu.SemaphoreType.DMA((8,)),
    ]
    grad = jax.ShapeDtypeStruct((DY, FF), F32)
    mixed, token_grads, prob_grads, grad_gate, grad_up, grad_down = pl.pallas_call(
        kernel,
        out_shape=(
            jax.ShapeDtypeStruct((TOK, D), BF),
            jax.ShapeDtypeStruct((TOK, D), BF),
            jax.ShapeDtypeStruct((8, GR), F32),
            grad, grad, grad,
        ),
        in_specs=[vmem] * 3 + [anywhere] * 3,
        out_specs=(vmem,) * 3 + (anywhere,) * 3,
        scratch_shapes=scratch,
        name="expert_layer",
        compiler_params=pltpu.CompilerParams(
            collective_id=0, has_side_effects=True, vmem_limit_bytes=67043328
        ),
    )(tokens, cotangent, meta, gate_proj[0], up_proj[0], down_proj[0])
    return (
        mixed, token_grads, prob_grads[:TOPK, :TOK].T,
        grad_gate[None], grad_up[None], grad_down[None],
    )


def solution(mesh):
    rows, weights = P(("dp", "expert"), None), P("expert", "dp", None)
    return jax.shard_map(
        layer,
        mesh=mesh,
        in_specs=(rows,) * 4 + (weights,) * 3,
        out_specs=(rows,) * 3 + (weights,) * 3,
        check_vma=False,
    )
```

```python
import jax
import jax.numpy as jnp
from jax import lax
from jax.experimental import pallas as pl
from jax.experimental.pallas import tpu as pltpu
from jax.sharding import PartitionSpec as P

MESH = pl.DeviceIdType.MESH
BF = jnp.bfloat16
F32 = jnp.float32
NY, NZ, NX, NC = 4, 8, 4, 2
TOK, D, FF, CAP, TOPK = 64, 2048, 768, 8, 6
ROWS = NX * NC * NZ * CAP
GR = 2 * TOK
DY = D // NY
HALF = DY // 2
NT = (((1,), (1,)), ((), ()))
TN = (((0,), (0,)), ((), ()))
VMEM_LIMIT = 57 * 1024 * 1024


def dot(a, b, dims=(((1,), (0,)), ((), ()))):
    return lax.dot_general(a, b, dims, preferred_element_type=F32)


def kernel(
    tok, cot, ids, probs, gw, uw, dw,
    mixed_o, tgrad_o, pg_o, og, ou, od,
    zt, zc, zm, xs_r, xs_g, rows, grads, gu, dn, gp, hid, dgu, xr_o, xr_d,
    meta, pm, wm, zs_o, zr_o, zs_d, zr_d, pgs, pgr, acc_o, acc_d,
    d1, d2, d3, dhp, dhm, dfp, dfm,
    g1, g2, g3, ghp, ghm, gfp, gfm,
    ssem, rsem, lsem,
):
    y = lax.axis_index("dp")
    e = lax.axis_index("expert")
    z, x, c = e // (NX * NC), (e // NC) % NX, e % NC

    def at(dy=0, dz=0, dx=0, dc=0):
        return (
            (y + dy + NY) % NY,
            ((z + dz + NZ) % NZ) * (NX * NC) + ((x + dx + NX) % NX) * NC + (c + dc) % NC,
        )

    yp, ym, zp, zq = at(dy=1), at(dy=-1), at(dz=1), at(dz=-1)
    offsets = [(k // NC, k % NC) for k in range(NX * NC)]
    to_x = [at(dx=dx, dc=dc) for dx, dc in offsets]
    from_x = [at(dx=-dx, dc=dc) for dx, dc in offsets]

    barrier = pltpu.get_barrier_semaphore()
    peers = [yp, ym, zp, zq] + to_x[1:]
    for peer in peers:
        pl.semaphore_signal(barrier, inc=1, device_id=peer, device_id_type=MESH)
    pl.semaphore_wait(barrier, len(peers))

    used = [0, 0]
    started = []

    def send(src, dst, peer):
        i = used[0]
        used[0] += 1
        copy = pltpu.make_async_remote_copy(
            src_ref=src, dst_ref=dst, send_sem=ssem.at[i], recv_sem=rsem.at[i],
            device_id=peer, device_id_type=MESH,
        )
        copy.start()
        started.append(copy)
        return copy

    def local(src, dst):
        i = used[1]
        used[1] += 1
        copy = pltpu.make_async_copy(src, dst, lsem.at[i])
        copy.start()
        return copy

    def yrows(dy, start=0, size=DY):
        return pl.ds(pl.multiple_of(((y + dy + NY) % NY) * DY + start, HALF), size)

    gcol, ucol = pl.ds(0, FF), pl.ds(FF, FF)

    lo, hi = pl.ds(0, HALF), pl.ds(HALF, HALF)

    def own(w, full, cols):
        first, second = full.at[yrows(0, 0, HALF), cols], full.at[yrows(0, HALF, HALF), cols]
        return (
            send(w.at[lo, :], first, yp),
            send(w.at[hi, :], second, ym),
            send(w.at[hi, :], second, yp),
            send(w.at[lo, :], first, ym),
        )

    def relay(parts, full, cols):
        parts[0].wait_recv()
        a = full.at[yrows(-1, 0, HALF), cols]
        first = send(a, a, yp)
        parts[1].wait_recv()
        b = full.at[yrows(1, HALF, HALF), cols]
        return first, send(b, b, ym), parts[2], parts[3]

    gate_own = own(gw, gu, gcol)
    up_own = own(uw, gu, ucol)

    def zblock(buf, j, zi, start=0, size=TOK):
        return buf.at[pl.ds(j * GR + zi * TOK + start, size), :]

    def zstep(buf, src, s):
        if s == 0:
            return send(src, zblock(buf, 0, 0), zp), send(src, zblock(buf, 0, 1), zq)
        if s < 3:
            return (
                send(zblock(buf, s - 1, 0), zblock(buf, s, 0), zp),
                send(zblock(buf, s - 1, 1), zblock(buf, s, 1), zq),
            )
        h = TOK // 2
        return (
            send(zblock(buf, 2, 0, 0, h), zblock(buf, 3, 1, 0, h), zp),
            send(zblock(buf, 2, 1, h, h), zblock(buf, 3, 1, h, h), zq),
        )

    def mstep(s):
        if s == 0:
            return send(meta, zm.at[0, 0], zp), send(meta, zm.at[0, 1], zq)
        if s < 3:
            return send(zm.at[s - 1, 0], zm.at[s, 0], zp), send(zm.at[s - 1, 1], zm.at[s, 1], zq)
        return (send(zm.at[2, 0], zm.at[3, 1], zp),)

    meta[...] = jnp.full(meta.shape, -1.0, F32)
    for start in (0, TOK):
        meta[0:TOPK, start : start + TOK] = ids[...].astype(F32)
        meta[8 : 8 + TOPK, start : start + TOK] = probs[...]
    m_now = mstep(0)
    t_now = zstep(zt, tok, 0)
    loads = [
        local(gw, gu.at[yrows(0), gcol]),
        local(uw, gu.at[yrows(0), ucol]),
        local(dw, dn.at[yrows(0), :]),
        local(tok, zblock(zt, 3, 0)),
        local(cot, zblock(zc, 3, 0)),
    ]
    zm[3, 0] = meta[...]

    row = lax.broadcasted_iota(jnp.int32, (GR, GR), 0)
    lane = lax.broadcasted_iota(jnp.int32, (GR, GR), 1)
    kk = row >> 4
    expert = (z * (NX * NC) + (((x + (kk >> 1)) & (NX - 1)) << 1) + ((c + kk) & 1)).astype(F32)
    slot = (row & (CAP - 1)).astype(F32)
    same_block = ((row >> 3) & 1) == (lane >> 6)
    earlier = jnp.where(((row >> 6) == (lane >> 6)) & (row < lane), 1.0, 0.0).astype(BF)
    low = lax.broadcasted_iota(jnp.int32, (16, GR), 1) < TOK

    def joined(j):
        return jnp.where(low, zm[j, 0], zm[j, 1])

    def route(j):
        both = joined(j)
        named = jnp.zeros((GR, GR), F32)
        weight = jnp.zeros((GR, GR), F32)
        for i in range(TOPK):
            hit = both[i : i + 1, :] == expert
            named = jnp.where(hit, 1.0, named)
            weight = weight + jnp.where(hit, both[8 + i : 9 + i, :], 0.0)
        rank = dot(named.astype(BF), earlier)
        fits = (named > 0.5) & (rank == slot) & same_block
        pm[j] = jnp.where(fits, 1.0, 0.0).astype(BF)
        wm[j] = jnp.where(fits, weight, 0.0)

    def group(buf, j):
        return buf.at[pl.ds(j * GR, GR), :]

    def piece(buf, j, k):
        return buf.at[pl.ds(j * GR + k * 16, 16), :]

    def xsend(src, dst, j, targets):
        return [send(piece(src, j, k), piece(dst, j, k), targets[k]) for k in range(1, NX * NC)]

    dispatched = []

    def dispatch_rows(j):
        filled = dot(pm[j], group(zt, j)[...]).astype(BF)
        group(xs_r, j)[...] = filled
        piece(rows, j, 0)[...] = filled[:16]
        dispatched.extend(xsend(xs_r, rows, j, to_x))

    def dispatch_grads(j):
        prob = jnp.sum(wm[j], axis=1, keepdims=True)
        filled = (dot(pm[j], group(zc, j)[...]) * prob).astype(BF)
        group(xs_g, j)[...] = filled
        piece(grads, j, 0)[...] = filled[:16]
        dispatched.extend(xsend(xs_g, grads, j, to_x))

    c_now = None
    gate_far = up_far = down_own = None
    for s in range(1, 5):
        t_next = m_next = None
        for copy in m_now:
            copy.wait_recv()
        if s < 4:
            m_now = mstep(s)
        for copy in t_now:
            copy.wait_recv()
        if s < 4:
            t_now = zstep(zt, tok, s)
        if s == 3:
            gate_far = relay(gate_own, gu, gcol)
        if s == 3:
            c_now = zstep(zc, cot, 0)
        if s == 4:
            loads[3].wait()
        route(s - 1)
        dispatch_rows(s - 1)
    loads[4].wait()
    for s in range(1, 5):
        for copy in c_now:
            copy.wait_recv()
        if s < 4:
            c_now = zstep(zc, cot, s)
        if s == 3:
            up_far = relay(up_own, gu, ucol)
            down_own = own(dw, dn, slice(None))
        dispatch_grads(s - 1)

    for copy in loads[:3]:
        copy.wait()
    for copy in dispatched[: 4 * 7]:
        copy.wait_recv()
    for copy in gate_far + up_far:
        copy.wait_recv()

    def forward_tile(n, carry):
        a = pl.ds(pl.multiple_of(n * 256, 256), 256)
        b = pl.ds(pl.multiple_of(n * 256 + FF, 256), 256)
        gate_pre = dot(rows[...], gu[:, a])
        gp[:, a] = gate_pre
        up_pre = dot(rows[...], gu[:, b])
        gp[:, b] = up_pre
        hid[:, a] = (gate_pre * (1.0 / (1.0 + jnp.exp(-gate_pre))) * up_pre).astype(BF)
        return carry

    lax.fori_loop(0, FF // 256, forward_tile, 0)
    for copy in dispatched[4 * 7 :]:
        copy.wait_recv()

    def term(src, rhs, dy, store):
        def tile(i, carry):
            cols = pl.ds(pl.multiple_of(((y + dy + NY) % NY) * DY + i * 256, 256), 256)
            store(pl.ds(pl.multiple_of(i * 256, 256), 256), dot(src[:, cols], rhs[...], TN))
            return carry

        lax.fori_loop(0, DY // 256, tile, 0)

    def into(buf):
        def store(where, value):
            buf[where, :] = value.astype(buf.dtype)

        return store

    def shares(src, rhs, s1, s2, s3, hp, hm, fp, fm, mine):
        term(src, rhs, 2, into(s2))
        half_p = send(s2.at[lo, :], hp, yp)
        half_m = send(s2.at[hi, :], hm, ym)
        term(src, rhs, 1, into(s1))
        early = [send(s1.at[hi, :], fp.at[hi, :], yp)]
        term(src, rhs, -1, into(s3))
        early.append(send(s3.at[lo, :], fm.at[lo, :], ym))
        term(src, rhs, 0, mine)
        return half_p, half_m, early

    def pass_on(state, s1, s3, hp, hm, fp, fm, cuts):
        half_p, half_m, early = state
        late = []
        for n, (start, size) in enumerate(cuts):
            cols = pl.ds(start, size)
            if n == 0:
                half_p.wait_recv()

            def add_p(i, carry, cols=cols):
                r = pl.ds(pl.multiple_of(i * 64, 64), 64)
                s1[r, cols] = (s1[r, cols].astype(F32) + hp[r, cols].astype(F32)).astype(BF)
                return carry

            lax.fori_loop(0, HALF // 64, add_p, 0)
            first = send(s1.at[lo, cols], fp.at[lo, cols], yp)
            if n == 0:
                half_m.wait_recv()

            def add_m(i, carry, cols=cols):
                r = pl.ds(pl.multiple_of(i * 64, 64), 64)
                t = pl.ds(pl.multiple_of(i * 64 + HALF, 64), 64)
                s3[t, cols] = (s3[t, cols].astype(F32) + hm[r, cols].astype(F32)).astype(BF)
                return carry

            lax.fori_loop(0, HALF // 64, add_m, 0)
            late.append((first, send(s3.at[hi, cols], fm.at[hi, cols], ym)))
        return early, late

    def finish(sent, cuts, fp, fm, outs):
        early, late = sent
        for copy in early:
            copy.wait_recv()
        for (start, size), pair, (out, at_col) in zip(cuts, late, outs):
            cols, mine = pl.ds(start, size), pl.ds(at_col, size)
            for copy in pair:
                copy.wait_recv()

            def add(i, carry, cols=cols, mine=mine, out=out):
                r = pl.ds(pl.multiple_of(i * 64, 64), 64)
                out[r, mine] = out[r, mine] + fp[r, cols].astype(F32) + fm[r, cols].astype(F32)
                return carry

            lax.fori_loop(0, DY // 64, add, 0)

    def gate_up(where, value):
        og[where, :] = value[:, :FF]
        ou[where, :] = value[:, FF:]

    down_cuts, gu_cuts = ((0, FF),), ((0, FF), (FF, 512), (FF + 512, 256))

    down_far = relay(down_own, dn, slice(None))
    down_state = shares(grads, hid, d1, d2, d3, dhp, dhm, dfp, dfm, into(od))
    for copy in down_far:
        copy.wait_recv()
    for copy in dispatched:
        copy.wait_send()

    def out_tile(n, carry):
        a = pl.ds(pl.multiple_of(n * 256, 256), 256)
        xs_r[:, a] = dot(hid[...], dn[a, :], NT).astype(BF)
        return carry

    lax.fori_loop(0, D // 256, out_tile, 0)
    back_o = {}
    for j in (3, 2, 1, 0):
        back_o[j] = xsend(xs_r, xr_o, j, from_x)
        piece(xr_o, j, 0)[...] = piece(xs_r, j, 0)[...]

    def backward_tile(n, carry):
        a = pl.ds(pl.multiple_of(n * 256, 256), 256)
        b = pl.ds(pl.multiple_of(n * 256 + FF, 256), 256)
        d_hidden = dot(grads[...], dn[:, a])
        gate_pre = gp[:, a]
        q = 1.0 / (1.0 + jnp.exp(-gate_pre))
        dgu[:, a] = (d_hidden * gp[:, b] * q * (1.0 + gate_pre * (1.0 - q))).astype(BF)
        dgu[:, b] = (d_hidden * (gate_pre * q)).astype(BF)
        return carry

    lax.fori_loop(0, FF // 256, backward_tile, 0)
    down_last = pass_on(down_state, d1, d3, dhp, dhm, dfp, dfm, down_cuts)
    gu_state = shares(rows, dgu, g1, g2, g3, ghp, ghm, gfp, gfm, gate_up)

    def d_rows_tile(n, carry):
        a = pl.ds(pl.multiple_of(n * 256, 256), 256)
        xs_g[:, a] = dot(dgu[...], gu[a, :], NT).astype(BF)
        return carry

    lax.fori_loop(0, D // 256, d_rows_tile, 0)
    back_d = {}
    for j in (3, 2, 1, 0):
        back_d[j] = xsend(xs_g, xr_d, j, from_x)
        piece(xr_d, j, 0)[...] = piece(xs_g, j, 0)[...]

    def ring(q, part, zs, zr, acc, prev):
        h = TOK // 2
        if q == 0:
            acc[...] = part[:TOK]
            zs[0, 0, :h] = part[TOK : TOK + h].astype(BF)
            zs[1, 0, :h] = part[TOK + h :].astype(BF)
            return (
                send(zs.at[0, 0, pl.ds(0, h)], zr.at[0, 0, pl.ds(0, h)], zp),
                send(zs.at[1, 0, pl.ds(0, h)], zr.at[1, 0, pl.ds(0, h)], zq),
            )
        p0, p1 = part[:TOK], part[TOK:]
        prev[0].wait_recv()
        if q == 1:
            zs[0, q, :h] = (p1[:h] + zr[0, 0, :h].astype(F32)).astype(BF)
            zs[0, q, h:] = p1[h:].astype(BF)
        else:
            zs[0, q] = (p1 + zr[0, q - 1].astype(F32)).astype(BF)
        first = send(zs.at[0, q], zr.at[0, q], zp)
        prev[1].wait_recv()
        if q == 1:
            zs[1, q, h:] = (p0[h:] + zr[1, 0, :h].astype(F32)).astype(BF)
            zs[1, q, :h] = p0[:h].astype(BF)
        else:
            zs[1, q] = (p0 + zr[1, q - 1].astype(F32)).astype(BF)
        return first, send(zs.at[1, q], zr.at[1, q], zq)

    def ring_small(q, part, prev):
        if q == 0:
            pgs[1, 0] = part
            pgs[0, 0] = part
            return (send(pgs.at[0, 0], pgr.at[0, 0], zp),)
        prev[0].wait_recv()
        pgs[0, q] = part + pgr[0, q - 1]
        first = send(pgs.at[0, q], pgr.at[0, q], zp)
        if q == 1:
            pgs[1, q] = part
        else:
            prev[1].wait_recv()
            pgs[1, q] = part + pgr[1, q - 1]
        return first, send(pgs.at[1, q], pgr.at[1, q], zq)

    ring_o = ring_p = ring_d = None
    for q in range(4):
        j = 3 - q
        for copy in back_o[j]:
            copy.wait_recv()
        returned = group(xr_o, j)[...]
        w = wm[j]
        w_hi = w.astype(BF)
        w_lo = (w - w_hi.astype(F32)).astype(BF)
        part = dot(w_hi, returned, TN) + dot(w_lo, returned, TN)
        ring_o = ring(q, part, zs_o, zr_o, acc_o, ring_o)
        scores = dot(returned, group(zc, j)[...], NT) * pm[j].astype(F32)
        both = joined(j)
        small = [
            jnp.sum(jnp.where(both[i : i + 1, :] == expert, scores, 0.0), axis=0, keepdims=True)
            for i in range(TOPK)
        ]
        small = jnp.concatenate(small + [jnp.zeros((2, GR), F32)], axis=0)
        ring_p = ring_small(q, small, ring_p)
    gu_last = pass_on(gu_state, g1, g3, ghp, ghm, gfp, gfm, gu_cuts)
    for q in range(4):
        j = 3 - q
        for copy in back_d[j]:
            copy.wait_recv()
        part = dot(pm[j], group(xr_d, j)[...], TN)
        ring_d = ring(q, part, zs_d, zr_d, acc_d, ring_d)

    for copy in ring_o + ring_p:
        copy.wait_recv()
    mixed_o[...] = (acc_o[...] + zr_o[0, 3].astype(F32) + zr_o[1, 3].astype(F32)).astype(BF)
    pg_o[...] = pgs[1, 0] + pgr[1, 3] + pltpu.roll(pgr[0, 3], TOK, 1)
    finish(down_last, down_cuts, dfp, dfm, ((od, 0),))
    for copy in ring_d:
        copy.wait_recv()
    tgrad_o[...] = (acc_d[...] + zr_d[0, 3].astype(F32) + zr_d[1, 3].astype(F32)).astype(BF)
    for copy in started:
        if not any(copy is other for other in dispatched + list(gu_late(gu_last))):
            copy.wait_send()
    finish(gu_last, gu_cuts, gfp, gfm, ((og, 0), (ou, 0), (ou, 512)))
    for copy in gu_late(gu_last):
        copy.wait_send()


def gu_late(sent):
    return [copy for pair in sent[1] for copy in pair]


def write_out(mixed, tgrad, pg, g, u, d, mixed_o, tgrad_o, pg_o, og, ou, od, sem):
    pairs = ((g, og), (u, ou), (d, od), (mixed, mixed_o), (tgrad, tgrad_o))
    copies = [pltpu.make_async_copy(src, dst, sem.at[i]) for i, (src, dst) in enumerate(pairs)]
    for copy in copies:
        copy.start()
    pg_o[...] = pg[:TOPK, :TOK]
    for copy in copies:
        copy.wait()


def layer(tokens, expert_ids, gate_probs, cotangent, gate_proj, up_proj, down_proj):
    vmem = pl.BlockSpec(memory_space=pltpu.VMEM)
    anywhere = pl.BlockSpec(memory_space=pl.ANY)
    v = pltpu.VMEM
    block = [v((DY, FF), BF)] * 3 + [v((HALF, FF), BF)] * 2 + [v((DY, FF), BF)] * 2
    wide = [v((DY, 2 * FF), BF)] * 3 + [v((HALF, 2 * FF), BF)] * 2 + [v((DY, 2 * FF), BF)] * 2
    scratch = [
        v((4 * GR, D), BF), v((4 * GR, D), BF), v((4, 2, 16, GR), F32),
        v((ROWS, D), BF), v((ROWS, D), BF), v((ROWS, D), BF), v((ROWS, D), BF),
        v((D, 2 * FF), BF), v((D, FF), BF),
        v((ROWS, 2 * FF), F32), v((ROWS, FF), BF), v((ROWS, 2 * FF), BF),
        v((ROWS, D), BF), v((ROWS, D), BF),
        v((16, GR), F32), v((4, GR, GR), BF), v((4, GR, GR), F32),
        v((2, 4, TOK, D), BF), v((2, 4, TOK, D), BF), v((2, 4, TOK, D), BF), v((2, 4, TOK, D), BF),
        v((2, 4, 8, GR), F32), v((2, 4, 8, GR), F32), v((TOK, D), F32), v((TOK, D), F32),
        *block, *wide,
        pltpu.SemaphoreType.DMA((208,)), pltpu.SemaphoreType.DMA((208,)), pltpu.SemaphoreType.DMA((8,)),
    ]
    shapes = [((TOK, D), BF), ((TOK, D), BF), ((8, GR), F32)] + [((DY, FF), F32)] * 3
    held = pl.pallas_call(
        kernel,
        out_shape=tuple(pltpu.VMEM(shape, dtype) for shape, dtype in shapes),
        in_specs=[vmem] * 4 + [anywhere] * 3,
        out_specs=(vmem,) * 6,
        scratch_shapes=scratch,
        name="expert_layer",
        compiler_params=pltpu.CompilerParams(
            collective_id=0, has_side_effects=True, vmem_limit_bytes=VMEM_LIMIT
        ),
    )(tokens, cotangent, expert_ids.T, gate_probs.T, gate_proj[0], up_proj[0], down_proj[0])
    shapes[2] = ((TOPK, TOK), F32)
    mixed, token_grads, prob_grads, grad_gate, grad_up, grad_down = pl.pallas_call(
        write_out,
        out_shape=tuple(jax.ShapeDtypeStruct(shape, dtype) for shape, dtype in shapes),
        in_specs=[vmem] * 6,
        out_specs=(anywhere, anywhere, vmem, anywhere, anywhere, anywhere),
        scratch_shapes=[pltpu.SemaphoreType.DMA((5,))],
        name="write_out",
        compiler_params=pltpu.CompilerParams(vmem_limit_bytes=1024 * 1024),
    )(*(pltpu.with_memory_space_constraint(part, pltpu.VMEM) for part in held))
    return (
        mixed, token_grads, prob_grads.T, grad_gate[None], grad_up[None], grad_down[None],
    )


def solution(mesh):
    rows, weights = P(("dp", "expert"), None), P("expert", "dp", None)
    return jax.shard_map(
        layer,
        mesh=mesh,
        in_specs=(rows,) * 4 + (weights,) * 3,
        out_specs=(rows,) * 3 + (weights,) * 3,
        check_vma=False,
    )
```

```python
import jax
import jax.numpy as jnp
from jax import lax
from jax.experimental import pallas as pl
from jax.experimental.pallas import tpu as pltpu
from jax.sharding import PartitionSpec as P

MESH = pl.DeviceIdType.MESH
BF = jnp.bfloat16
F32 = jnp.float32
NY, NZ, NX, NC = 4, 8, 4, 2
TOK, D, FF, CAP, TOPK = 64, 2048, 768, 8, 6
ROWS = NX * NC * NZ * CAP
GR = 2 * TOK
DY = D // NY
HALF = DY // 2
NT = (((1,), (1,)), ((), ()))
TN = (((0,), (0,)), ((), ()))
VMEM_LIMIT = 57 * 1024 * 1024


def dot(a, b, dims=(((1,), (0,)), ((), ()))):
    return lax.dot_general(a, b, dims, preferred_element_type=F32)


def kernel(
    tok, cot, ids, probs, gw, uw, dw,
    mixed_o, tgrad_o, pg_o, og, ou, od,
    zt, zc, zm, xs_r, xs_g, rows, grads, gu, dn, gp, hid, dgu, xr_o, xr_d,
    meta, pm, wm, zs_o, zr_o, zs_d, zr_d, pgs, pgr, acc_o, acc_d,
    d1, d2, d3, dhp, dhm, dfp, dfm,
    g1, g2, g3, ghp, ghm, gfp, gfm,
    ids_v, probs_v, go, ssem, rsem, lsem,
):
    y = lax.axis_index("dp")
    e = lax.axis_index("expert")
    z, x, c = e // (NX * NC), (e // NC) % NX, e % NC

    def at(dy=0, dz=0, dx=0, dc=0):
        return (
            (y + dy + NY) % NY,
            ((z + dz + NZ) % NZ) * (NX * NC) + ((x + dx + NX) % NX) * NC + (c + dc) % NC,
        )

    yp, ym, zp, zq = at(dy=1), at(dy=-1), at(dz=1), at(dz=-1)
    offsets = [(k // NC, k % NC) for k in range(NX * NC)]
    to_x = [at(dx=dx, dc=dc) for dx, dc in offsets]
    from_x = [at(dx=-dx, dc=dc) for dx, dc in offsets]

    barrier = pltpu.get_barrier_semaphore()

    def tell(peer):
        pl.semaphore_signal(barrier, inc=1, device_id=peer, device_id_type=MESH)

    other, first, second = at(dc=1), (NC - c) % NC, 1 - c
    for dy in (1, -1):
        tell(at(dy=dy, dc=first))
    for dz in (1, -1):
        tell(at(dz=dz, dc=second))
    for dx in range(1, NX):
        tell(at(dx=dx, dc=second))
    tell(other)

    @pl.when(c == 0)
    def _():
        pl.semaphore_wait(barrier, NC * 2 + 1)
        pl.semaphore_signal(go, inc=1, device_id=other, device_id_type=MESH)

    @pl.when(c == 1)
    def _():
        pl.semaphore_wait(go, 1)

    used = [0, 0]
    started = []

    def send(src, dst, peer):
        i = used[0]
        used[0] += 1
        copy = pltpu.make_async_remote_copy(
            src_ref=src, dst_ref=dst, send_sem=ssem.at[i], recv_sem=rsem.at[i],
            device_id=peer, device_id_type=MESH,
        )
        copy.start()
        started.append(copy)
        return copy

    def local(src, dst):
        i = used[1]
        used[1] += 1
        copy = pltpu.make_async_copy(src, dst, lsem.at[i])
        copy.start()
        return copy

    def yrows(dy, start=0, size=DY):
        return pl.ds(pl.multiple_of(((y + dy + NY) % NY) * DY + start, HALF), size)

    gcol, ucol = pl.ds(0, FF), pl.ds(FF, FF)

    lo, hi = pl.ds(0, HALF), pl.ds(HALF, HALF)

    def own(w, full, cols):
        first, second = full.at[yrows(0, 0, HALF), cols], full.at[yrows(0, HALF, HALF), cols]
        return (
            send(w.at[lo, :], first, yp),
            send(w.at[hi, :], second, ym),
            send(w.at[hi, :], second, yp),
            send(w.at[lo, :], first, ym),
        )

    def relay(parts, full, cols):
        parts[0].wait_recv()
        a = full.at[yrows(-1, 0, HALF), cols]
        first = send(a, a, yp)
        parts[1].wait_recv()
        b = full.at[yrows(1, HALF, HALF), cols]
        return first, send(b, b, ym), parts[2], parts[3]

    gate_own = own(gw, gu, gcol)
    up_own = own(uw, gu, ucol)
    tables = [local(ids, ids_v), local(probs, probs_v)]

    def zblock(buf, j, zi, start=0, size=TOK):
        return buf.at[pl.ds(j * GR + zi * TOK + start, size), :]

    def zstep(buf, src, s):
        if s == 0:
            return send(src, zblock(buf, 0, 0), zp), send(src, zblock(buf, 0, 1), zq)
        if s < 3:
            return (
                send(zblock(buf, s - 1, 0), zblock(buf, s, 0), zp),
                send(zblock(buf, s - 1, 1), zblock(buf, s, 1), zq),
            )
        h = TOK // 2
        return (
            send(zblock(buf, 2, 0, 0, h), zblock(buf, 3, 1, 0, h), zp),
            send(zblock(buf, 2, 1, h, h), zblock(buf, 3, 1, h, h), zq),
        )

    def mstep(s):
        if s == 0:
            return send(meta, zm.at[0, 0], zp), send(meta, zm.at[0, 1], zq)
        if s < 3:
            return send(zm.at[s - 1, 0], zm.at[s, 0], zp), send(zm.at[s - 1, 1], zm.at[s, 1], zq)
        return (send(zm.at[2, 0], zm.at[3, 1], zp),)

    for copy in tables:
        copy.wait()
    meta[...] = jnp.full(meta.shape, -1.0, F32)
    for start in (0, TOK):
        meta[0:TOPK, start : start + TOK] = ids_v[...].astype(F32)
        meta[8 : 8 + TOPK, start : start + TOK] = probs_v[...]

    @pl.when(c == 1)
    def _():
        pl.semaphore_wait(barrier, 1 + NC * 2 + NC * (NX - 1))
        pl.semaphore_signal(go, inc=1, device_id=other, device_id_type=MESH)

    @pl.when(c == 0)
    def _():
        pl.semaphore_wait(go, 1)

    m_now = mstep(0)
    t_now = zstep(zt, tok, 0)
    loads = [
        local(gw, gu.at[yrows(0), gcol]),
        local(uw, gu.at[yrows(0), ucol]),
        local(dw, dn.at[yrows(0), :]),
        local(tok, zblock(zt, 3, 0)),
        local(cot, zblock(zc, 3, 0)),
    ]
    zm[3, 0] = meta[...]

    row = lax.broadcasted_iota(jnp.int32, (GR, GR), 0)
    lane = lax.broadcasted_iota(jnp.int32, (GR, GR), 1)
    kk = row >> 4
    expert = (z * (NX * NC) + (((x + (kk >> 1)) & (NX - 1)) << 1) + ((c + kk) & 1)).astype(F32)
    slot = (row & (CAP - 1)).astype(F32)
    same_block = ((row >> 3) & 1) == (lane >> 6)
    earlier = jnp.where(((row >> 6) == (lane >> 6)) & (row < lane), 1.0, 0.0).astype(BF)
    low = lax.broadcasted_iota(jnp.int32, (16, GR), 1) < TOK

    def joined(j):
        return jnp.where(low, zm[j, 0], zm[j, 1])

    def route(j):
        both = joined(j)
        named = jnp.zeros((GR, GR), F32)
        weight = jnp.zeros((GR, GR), F32)
        for i in range(TOPK):
            hit = both[i : i + 1, :] == expert
            named = jnp.where(hit, 1.0, named)
            weight = weight + jnp.where(hit, both[8 + i : 9 + i, :], 0.0)
        rank = dot(named.astype(BF), earlier)
        fits = (named > 0.5) & (rank == slot) & same_block
        pm[j] = jnp.where(fits, 1.0, 0.0).astype(BF)
        wm[j] = jnp.where(fits, weight, 0.0)

    def group(buf, j):
        return buf.at[pl.ds(j * GR, GR), :]

    def piece(buf, j, k):
        return buf.at[pl.ds(j * GR + k * 16, 16), :]

    def xsend(src, dst, j, targets):
        return [send(piece(src, j, k), piece(dst, j, k), targets[k]) for k in range(1, NX * NC)]

    dispatched = []

    def dispatch_rows(j):
        filled = dot(pm[j], group(zt, j)[...]).astype(BF)
        group(xs_r, j)[...] = filled
        piece(rows, j, 0)[...] = filled[:16]
        dispatched.extend(xsend(xs_r, rows, j, to_x))

    def dispatch_grads(j):
        prob = jnp.sum(wm[j], axis=1, keepdims=True)
        filled = (dot(pm[j], group(zc, j)[...]) * prob).astype(BF)
        group(xs_g, j)[...] = filled
        piece(grads, j, 0)[...] = filled[:16]
        dispatched.extend(xsend(xs_g, grads, j, to_x))

    c_now = None
    gate_far = up_far = down_own = None
    for s in range(1, 5):
        t_next = m_next = None
        for copy in m_now:
            copy.wait_recv()
        if s < 4:
            m_now = mstep(s)
        for copy in t_now:
            copy.wait_recv()
        if s < 4:
            t_now = zstep(zt, tok, s)
        if s == 3:
            gate_far = relay(gate_own, gu, gcol)
        if s == 3:
            c_now = zstep(zc, cot, 0)
        if s == 4:
            loads[3].wait()
        route(s - 1)
        dispatch_rows(s - 1)
    loads[4].wait()
    for s in range(1, 5):
        for copy in c_now:
            copy.wait_recv()
        if s < 4:
            c_now = zstep(zc, cot, s)
        if s == 1:
            up_far = relay(up_own, gu, ucol)
            down_own = own(dw, dn, slice(None))
        dispatch_grads(s - 1)

    for copy in loads[:3]:
        copy.wait()
    for copy in dispatched[: 4 * 7]:
        copy.wait_recv()
    for copy in gate_far + up_far:
        copy.wait_recv()

    def forward_tile(n, carry):
        a = pl.ds(pl.multiple_of(n * 256, 256), 256)
        b = pl.ds(pl.multiple_of(n * 256 + FF, 256), 256)
        gate_pre = dot(rows[...], gu[:, a])
        gp[:, a] = gate_pre
        up_pre = dot(rows[...], gu[:, b])
        gp[:, b] = up_pre
        hid[:, a] = (gate_pre * (1.0 / (1.0 + jnp.exp(-gate_pre))) * up_pre).astype(BF)
        return carry

    lax.fori_loop(0, FF // 256, forward_tile, 0)
    for copy in dispatched[4 * 7 :]:
        copy.wait_recv()

    def term(src, rhs, dy, store):
        def tile(i, carry):
            cols = pl.ds(pl.multiple_of(((y + dy + NY) % NY) * DY + i * 256, 256), 256)
            store(pl.ds(pl.multiple_of(i * 256, 256), 256), dot(src[:, cols], rhs[...], TN))
            return carry

        lax.fori_loop(0, DY // 256, tile, 0)

    def into(buf):
        def store(where, value):
            buf[where, :] = value.astype(buf.dtype)

        return store

    def shares(src, rhs, s1, s2, s3, hp, hm, fp, fm, mine):
        term(src, rhs, 2, into(s2))
        half_p = send(s2.at[lo, :], hp, yp)
        half_m = send(s2.at[hi, :], hm, ym)
        term(src, rhs, 1, into(s1))
        early = [send(s1.at[hi, :], fp.at[hi, :], yp)]
        term(src, rhs, -1, into(s3))
        early.append(send(s3.at[lo, :], fm.at[lo, :], ym))
        term(src, rhs, 0, mine)
        return half_p, half_m, early

    def pass_on(state, s1, s3, hp, hm, fp, fm, cuts):
        half_p, half_m, early = state
        late = []
        for n, (start, size) in enumerate(cuts):
            cols = pl.ds(start, size)
            if n == 0:
                half_p.wait_recv()

            def add_p(i, carry, cols=cols):
                r = pl.ds(pl.multiple_of(i * 64, 64), 64)
                s1[r, cols] = (s1[r, cols].astype(F32) + hp[r, cols].astype(F32)).astype(BF)
                return carry

            lax.fori_loop(0, HALF // 64, add_p, 0)
            first = send(s1.at[lo, cols], fp.at[lo, cols], yp)
            if n == 0:
                half_m.wait_recv()

            def add_m(i, carry, cols=cols):
                r = pl.ds(pl.multiple_of(i * 64, 64), 64)
                t = pl.ds(pl.multiple_of(i * 64 + HALF, 64), 64)
                s3[t, cols] = (s3[t, cols].astype(F32) + hm[r, cols].astype(F32)).astype(BF)
                return carry

            lax.fori_loop(0, HALF // 64, add_m, 0)
            late.append((first, send(s3.at[hi, cols], fm.at[hi, cols], ym)))
        return early, late

    def finish(sent, cuts, fp, fm, outs):
        early, late = sent
        for copy in early:
            copy.wait_recv()
        for (start, size), pair, (out, at_col) in zip(cuts, late, outs):
            cols, mine = pl.ds(start, size), pl.ds(at_col, size)
            for copy in pair:
                copy.wait_recv()

            def add(i, carry, cols=cols, mine=mine, out=out):
                r = pl.ds(pl.multiple_of(i * 64, 64), 64)
                out[r, mine] = out[r, mine] + fp[r, cols].astype(F32) + fm[r, cols].astype(F32)
                return carry

            lax.fori_loop(0, DY // 64, add, 0)

    def gate_up(where, value):
        og[where, :] = value[:, :FF]
        ou[where, :] = value[:, FF:]

    down_cuts, gu_cuts = ((0, FF),), ((0, FF), (FF, 512), (FF + 512, 256))

    down_far = relay(down_own, dn, slice(None))
    down_state = shares(grads, hid, d1, d2, d3, dhp, dhm, dfp, dfm, into(od))
    for copy in down_far:
        copy.wait_recv()
    for copy in dispatched:
        copy.wait_send()

    def out_tile(n, carry):
        a = pl.ds(pl.multiple_of(n * 256, 256), 256)
        xs_r[:, a] = dot(hid[...], dn[a, :], NT).astype(BF)
        return carry

    lax.fori_loop(0, D // 256, out_tile, 0)
    back_o = {}
    for j in (3, 2, 1, 0):
        back_o[j] = xsend(xs_r, xr_o, j, from_x)
        piece(xr_o, j, 0)[...] = piece(xs_r, j, 0)[...]

    def backward_tile(n, carry):
        a = pl.ds(pl.multiple_of(n * 256, 256), 256)
        b = pl.ds(pl.multiple_of(n * 256 + FF, 256), 256)
        d_hidden = dot(grads[...], dn[:, a])
        gate_pre = gp[:, a]
        q = 1.0 / (1.0 + jnp.exp(-gate_pre))
        dgu[:, a] = (d_hidden * gp[:, b] * q * (1.0 + gate_pre * (1.0 - q))).astype(BF)
        dgu[:, b] = (d_hidden * (gate_pre * q)).astype(BF)
        return carry

    lax.fori_loop(0, FF // 256, backward_tile, 0)
    down_last = pass_on(down_state, d1, d3, dhp, dhm, dfp, dfm, down_cuts)
    gu_state = shares(rows, dgu, g1, g2, g3, ghp, ghm, gfp, gfm, gate_up)

    def d_rows_tile(n, carry):
        a = pl.ds(pl.multiple_of(n * 256, 256), 256)
        xs_g[:, a] = dot(dgu[...], gu[a, :], NT).astype(BF)
        return carry

    lax.fori_loop(0, D // 256, d_rows_tile, 0)
    back_d = {}
    for j in (3, 2, 1, 0):
        back_d[j] = xsend(xs_g, xr_d, j, from_x)
        piece(xr_d, j, 0)[...] = piece(xs_g, j, 0)[...]

    def ring(q, part, zs, zr, acc, prev):
        h = TOK // 2
        if q == 0:
            acc[...] = part[:TOK]
            zs[0, 0, :h] = part[TOK : TOK + h].astype(BF)
            zs[1, 0, :h] = part[TOK + h :].astype(BF)
            return (
                send(zs.at[0, 0, pl.ds(0, h)], zr.at[0, 0, pl.ds(0, h)], zp),
                send(zs.at[1, 0, pl.ds(0, h)], zr.at[1, 0, pl.ds(0, h)], zq),
            )
        p0, p1 = part[:TOK], part[TOK:]
        prev[0].wait_recv()
        if q == 1:
            zs[0, q, :h] = (p1[:h] + zr[0, 0, :h].astype(F32)).astype(BF)
            zs[0, q, h:] = p1[h:].astype(BF)
        else:
            zs[0, q] = (p1 + zr[0, q - 1].astype(F32)).astype(BF)
        first = send(zs.at[0, q], zr.at[0, q], zp)
        prev[1].wait_recv()
        if q == 1:
            zs[1, q, h:] = (p0[h:] + zr[1, 0, :h].astype(F32)).astype(BF)
            zs[1, q, :h] = p0[:h].astype(BF)
        else:
            zs[1, q] = (p0 + zr[1, q - 1].astype(F32)).astype(BF)
        return first, send(zs.at[1, q], zr.at[1, q], zq)

    def ring_small(q, part, prev):
        if q == 0:
            pgs[1, 0] = part
            pgs[0, 0] = part
            return (send(pgs.at[0, 0], pgr.at[0, 0], zp),)
        prev[0].wait_recv()
        pgs[0, q] = part + pgr[0, q - 1]
        first = send(pgs.at[0, q], pgr.at[0, q], zp)
        if q == 1:
            pgs[1, q] = part
        else:
            prev[1].wait_recv()
            pgs[1, q] = part + pgr[1, q - 1]
        return first, send(pgs.at[1, q], pgr.at[1, q], zq)

    ring_o = ring_p = ring_d = None
    for q in range(4):
        j = 3 - q
        for copy in back_o[j]:
            copy.wait_recv()
        returned = group(xr_o, j)[...]
        w = wm[j]
        w_hi = w.astype(BF)
        w_lo = (w - w_hi.astype(F32)).astype(BF)
        part = dot(w_hi, returned, TN) + dot(w_lo, returned, TN)
        ring_o = ring(q, part, zs_o, zr_o, acc_o, ring_o)
        scores = dot(returned, group(zc, j)[...], NT) * pm[j].astype(F32)
        both = joined(j)
        small = [
            jnp.sum(jnp.where(both[i : i + 1, :] == expert, scores, 0.0), axis=0, keepdims=True)
            for i in range(TOPK)
        ]
        small = jnp.concatenate(small + [jnp.zeros((2, GR), F32)], axis=0)
        ring_p = ring_small(q, small, ring_p)
    gu_last = pass_on(gu_state, g1, g3, ghp, ghm, gfp, gfm, gu_cuts)
    for q in range(4):
        j = 3 - q
        for copy in back_d[j]:
            copy.wait_recv()
        part = dot(pm[j], group(xr_d, j)[...], TN)
        ring_d = ring(q, part, zs_d, zr_d, acc_d, ring_d)

    for copy in ring_o + ring_p:
        copy.wait_recv()
    mixed_o[...] = (acc_o[...] + zr_o[0, 3].astype(F32) + zr_o[1, 3].astype(F32)).astype(BF)
    pg_o[...] = pgs[1, 0] + pgr[1, 3] + pltpu.roll(pgr[0, 3], TOK, 1)
    finish(down_last, down_cuts, dfp, dfm, ((od, 0),))
    for copy in ring_d:
        copy.wait_recv()
    tgrad_o[...] = (acc_d[...] + zr_d[0, 3].astype(F32) + zr_d[1, 3].astype(F32)).astype(BF)
    for copy in started:
        if not any(copy is other for other in dispatched + list(gu_late(gu_last))):
            copy.wait_send()
    finish(gu_last, gu_cuts, gfp, gfm, ((og, 0), (ou, 0), (ou, 512)))
    for copy in gu_late(gu_last):
        copy.wait_send()


def gu_late(sent):
    return [copy for pair in sent[1] for copy in pair]


def write_out(mixed, tgrad, pg, g, u, d, mixed_o, tgrad_o, pg_o, og, ou, od, sem):
    pairs = ((g, og), (u, ou), (d, od), (mixed, mixed_o), (tgrad, tgrad_o))
    copies = [pltpu.make_async_copy(src, dst, sem.at[i]) for i, (src, dst) in enumerate(pairs)]
    for copy in copies:
        copy.start()
    pg_o[...] = pg[:TOPK, :TOK]
    for copy in copies:
        copy.wait()


def layer(tokens, expert_ids, gate_probs, cotangent, gate_proj, up_proj, down_proj):
    vmem = pl.BlockSpec(memory_space=pltpu.VMEM)
    anywhere = pl.BlockSpec(memory_space=pl.ANY)
    v = pltpu.VMEM
    block = [v((DY, FF), BF)] * 3 + [v((HALF, FF), BF)] * 2 + [v((DY, FF), BF)] * 2
    wide = [v((DY, 2 * FF), BF)] * 3 + [v((HALF, 2 * FF), BF)] * 2 + [v((DY, 2 * FF), BF)] * 2
    scratch = [
        v((4 * GR, D), BF), v((4 * GR, D), BF), v((4, 2, 16, GR), F32),
        v((ROWS, D), BF), v((ROWS, D), BF), v((ROWS, D), BF), v((ROWS, D), BF),
        v((D, 2 * FF), BF), v((D, FF), BF),
        v((ROWS, 2 * FF), F32), v((ROWS, FF), BF), v((ROWS, 2 * FF), BF),
        v((ROWS, D), BF), v((ROWS, D), BF),
        v((16, GR), F32), v((4, GR, GR), BF), v((4, GR, GR), F32),
        v((2, 4, TOK, D), BF), v((2, 4, TOK, D), BF), v((2, 4, TOK, D), BF), v((2, 4, TOK, D), BF),
        v((2, 4, 8, GR), F32), v((2, 4, 8, GR), F32), v((TOK, D), F32), v((TOK, D), F32),
        *block, *wide,
        v((TOPK, TOK), jnp.int32), v((TOPK, TOK), F32), pltpu.SemaphoreType.REGULAR,
        pltpu.SemaphoreType.DMA((208,)), pltpu.SemaphoreType.DMA((208,)), pltpu.SemaphoreType.DMA((8,)),
    ]
    shapes = [((TOK, D), BF), ((TOK, D), BF), ((8, GR), F32)] + [((DY, FF), F32)] * 3
    held = pl.pallas_call(
        kernel,
        out_shape=tuple(pltpu.VMEM(shape, dtype) for shape, dtype in shapes),
        in_specs=[vmem] * 4 + [anywhere] * 3,
        out_specs=(vmem,) * 6,
        scratch_shapes=scratch,
        name="expert_layer",
        compiler_params=pltpu.CompilerParams(
            collective_id=0, has_side_effects=True, vmem_limit_bytes=VMEM_LIMIT
        ),
    )(tokens, cotangent, expert_ids.T, gate_probs.T, gate_proj[0], up_proj[0], down_proj[0])
    shapes[2] = ((TOPK, TOK), F32)
    mixed, token_grads, prob_grads, grad_gate, grad_up, grad_down = pl.pallas_call(
        write_out,
        out_shape=tuple(jax.ShapeDtypeStruct(shape, dtype) for shape, dtype in shapes),
        in_specs=[vmem] * 6,
        out_specs=(anywhere, anywhere, vmem, anywhere, anywhere, anywhere),
        scratch_shapes=[pltpu.SemaphoreType.DMA((5,))],
        name="write_out",
        compiler_params=pltpu.CompilerParams(vmem_limit_bytes=1024 * 1024),
    )(*(pltpu.with_memory_space_constraint(part, pltpu.VMEM) for part in held))
    return (
        mixed, token_grads, prob_grads.T, grad_gate[None], grad_up[None], grad_down[None],
    )


def solution(mesh):
    rows, weights = P(("dp", "expert"), None), P("expert", "dp", None)
    return jax.shard_map(
        layer,
        mesh=mesh,
        in_specs=(rows,) * 4 + (weights,) * 3,
        out_specs=(rows,) * 3 + (weights,) * 3,
        check_vma=False,
    )
```

```python
import jax
import jax.numpy as jnp
from jax import lax
from jax.experimental import pallas as pl
from jax.experimental.pallas import tpu as pltpu
from jax.sharding import PartitionSpec as P

MESH = pl.DeviceIdType.MESH
BF = jnp.bfloat16
F32 = jnp.float32
NY, NZ, NX, NC = 4, 8, 4, 2
TOK, D, FF, CAP, TOPK = 64, 2048, 768, 8, 6
ROWS = NX * NC * NZ * CAP
GR = 2 * TOK
DY = D // NY
HALF = DY // 2
NT = (((1,), (1,)), ((), ()))
TN = (((0,), (0,)), ((), ()))
VMEM_LIMIT = 57 * 1024 * 1024


def dot(a, b, dims=(((1,), (0,)), ((), ()))):
    return lax.dot_general(a, b, dims, preferred_element_type=F32)


def kernel(
    tok, cot, ids, probs, gw, uw, dw,
    mixed_o, tgrad_o, pg_o, og, ou, od,
    zt, zc, zm, xs_r, xs_g, rows, grads, gu, dn, gp, hid, dgu, xr_o, xr_d,
    meta, pm, wm, zs_o, zr_o, zs_d, zr_d, pgs, pgr, acc_o, acc_d,
    d1, d2, d3, dhp, dhm, dfp, dfm,
    g1, g2, g3, ghp, ghm, gfp, gfm,
    ids_v, probs_v, go, ssem, rsem, lsem,
):
    y = lax.axis_index("dp")
    e = lax.axis_index("expert")
    z, x, c = e // (NX * NC), (e // NC) % NX, e % NC

    def at(dy=0, dz=0, dx=0, dc=0):
        return (
            (y + dy + NY) % NY,
            ((z + dz + NZ) % NZ) * (NX * NC) + ((x + dx + NX) % NX) * NC + (c + dc) % NC,
        )

    yp, ym, zp, zq = at(dy=1), at(dy=-1), at(dz=1), at(dz=-1)
    offsets = [(k // NC, k % NC) for k in range(NX * NC)]
    to_x = [at(dx=dx, dc=dc) for dx, dc in offsets]
    from_x = [at(dx=-dx, dc=dc) for dx, dc in offsets]

    barrier = pltpu.get_barrier_semaphore()

    def tell(peer):
        pl.semaphore_signal(barrier, inc=1, device_id=peer, device_id_type=MESH)

    other, first, second = at(dc=1), (NC - c) % NC, 1 - c
    for dy in (1, -1):
        tell(at(dy=dy, dc=first))
    for dz in (1, -1):
        tell(at(dz=dz, dc=second))
    for dx in range(1, NX):
        tell(at(dx=dx, dc=second))
    tell(other)

    @pl.when(c == 0)
    def _():
        pl.semaphore_wait(barrier, NC * 2 + 1)
        pl.semaphore_signal(go, inc=1, device_id=other, device_id_type=MESH)

    @pl.when(c == 1)
    def _():
        pl.semaphore_wait(go, 1)

    used = [0, 0]
    started = []

    def send(src, dst, peer):
        i = used[0]
        used[0] += 1
        copy = pltpu.make_async_remote_copy(
            src_ref=src, dst_ref=dst, send_sem=ssem.at[i], recv_sem=rsem.at[i],
            device_id=peer, device_id_type=MESH,
        )
        copy.start()
        started.append(copy)
        return copy

    def local(src, dst):
        i = used[1]
        used[1] += 1
        copy = pltpu.make_async_copy(src, dst, lsem.at[i])
        copy.start()
        return copy

    def yrows(dy, start=0, size=DY):
        return pl.ds(pl.multiple_of(((y + dy + NY) % NY) * DY + start, HALF), size)

    gcol, ucol = pl.ds(0, FF), pl.ds(FF, FF)

    lo, hi = pl.ds(0, HALF), pl.ds(HALF, HALF)

    def own(w, full, cols):
        first, second = full.at[yrows(0, 0, HALF), cols], full.at[yrows(0, HALF, HALF), cols]
        return (
            send(w.at[lo, :], first, yp),
            send(w.at[hi, :], second, ym),
            send(w.at[hi, :], second, yp),
            send(w.at[lo, :], first, ym),
        )

    def relay(parts, full, cols):
        parts[0].wait_recv()
        a = full.at[yrows(-1, 0, HALF), cols]
        first = send(a, a, yp)
        parts[1].wait_recv()
        b = full.at[yrows(1, HALF, HALF), cols]
        return first, send(b, b, ym), parts[2], parts[3]

    gate_own = own(gw, gu, gcol)
    up_own = own(uw, gu, ucol)
    tables = [local(ids, ids_v), local(probs, probs_v)]

    def zblock(buf, j, zi, start=0, size=TOK):
        return buf.at[pl.ds(j * GR + zi * TOK + start, size), :]

    def zstep(buf, src, s):
        if s == 0:
            return send(src, zblock(buf, 0, 0), zp), send(src, zblock(buf, 0, 1), zq)
        if s < 3:
            return (
                send(zblock(buf, s - 1, 0), zblock(buf, s, 0), zp),
                send(zblock(buf, s - 1, 1), zblock(buf, s, 1), zq),
            )
        h = TOK // 2
        return (
            send(zblock(buf, 2, 0, 0, h), zblock(buf, 3, 1, 0, h), zp),
            send(zblock(buf, 2, 1, h, h), zblock(buf, 3, 1, h, h), zq),
        )

    def mstep(s):
        if s == 0:
            return send(meta, zm.at[0, 0], zp), send(meta, zm.at[0, 1], zq)
        if s < 3:
            return send(zm.at[s - 1, 0], zm.at[s, 0], zp), send(zm.at[s - 1, 1], zm.at[s, 1], zq)
        return (send(zm.at[2, 0], zm.at[3, 1], zp),)

    for copy in tables:
        copy.wait()
    meta[...] = jnp.full(meta.shape, -1.0, F32)
    for start in (0, TOK):
        meta[0:TOPK, start : start + TOK] = ids_v[...].astype(F32)
        meta[8 : 8 + TOPK, start : start + TOK] = probs_v[...]

    @pl.when(c == 1)
    def _():
        pl.semaphore_wait(barrier, 1 + NC * 2 + NC * (NX - 1))
        pl.semaphore_signal(go, inc=1, device_id=other, device_id_type=MESH)

    @pl.when(c == 0)
    def _():
        pl.semaphore_wait(go, 1)

    m_now = mstep(0)
    t_now = zstep(zt, tok, 0)
    loads = [
        local(gw, gu.at[yrows(0), gcol]),
        local(uw, gu.at[yrows(0), ucol]),
        local(dw, dn.at[yrows(0), :]),
        local(tok, zblock(zt, 3, 0)),
        local(cot, zblock(zc, 3, 0)),
    ]
    zm[3, 0] = meta[...]

    row = lax.broadcasted_iota(jnp.int32, (GR, GR), 0)
    lane = lax.broadcasted_iota(jnp.int32, (GR, GR), 1)
    kk = row >> 4
    expert = (z * (NX * NC) + (((x + (kk >> 1)) & (NX - 1)) << 1) + ((c + kk) & 1)).astype(F32)
    slot = (row & (CAP - 1)).astype(F32)
    same_block = ((row >> 3) & 1) == (lane >> 6)
    earlier = jnp.where(((row >> 6) == (lane >> 6)) & (row < lane), 1.0, 0.0).astype(BF)
    low = lax.broadcasted_iota(jnp.int32, (16, GR), 1) < TOK

    def joined(j):
        return jnp.where(low, zm[j, 0], zm[j, 1])

    def route(j):
        both = joined(j)
        named = jnp.zeros((GR, GR), F32)
        weight = jnp.zeros((GR, GR), F32)
        for i in range(TOPK):
            hit = both[i : i + 1, :] == expert
            named = jnp.where(hit, 1.0, named)
            weight = weight + jnp.where(hit, both[8 + i : 9 + i, :], 0.0)
        rank = dot(named.astype(BF), earlier)
        fits = (named > 0.5) & (rank == slot) & same_block
        pm[j] = jnp.where(fits, 1.0, 0.0).astype(BF)
        wm[j] = jnp.where(fits, weight, 0.0)

    def group(buf, j):
        return buf.at[pl.ds(j * GR, GR), :]

    def piece(buf, j, k):
        return buf.at[pl.ds(j * GR + k * 16, 16), :]

    def xsend(src, dst, j, targets):
        return [send(piece(src, j, k), piece(dst, j, k), targets[k]) for k in range(1, NX * NC)]

    dispatched = []

    def dispatch_rows(j):
        filled = dot(pm[j], group(zt, j)[...]).astype(BF)
        group(xs_r, j)[...] = filled
        piece(rows, j, 0)[...] = filled[:16]
        dispatched.extend(xsend(xs_r, rows, j, to_x))

    def dispatch_grads(j):
        prob = jnp.sum(wm[j], axis=1, keepdims=True)
        filled = (dot(pm[j], group(zc, j)[...]) * prob).astype(BF)
        group(xs_g, j)[...] = filled
        piece(grads, j, 0)[...] = filled[:16]
        dispatched.extend(xsend(xs_g, grads, j, to_x))

    c_now = None
    gate_far = up_far = down_own = None
    for s in range(1, 5):
        t_next = m_next = None
        for copy in m_now:
            copy.wait_recv()
        if s < 4:
            m_now = mstep(s)
        for copy in t_now:
            copy.wait_recv()
        if s < 4:
            t_now = zstep(zt, tok, s)
        if s == 3:
            gate_far = relay(gate_own, gu, gcol)
        if s == 3:
            c_now = zstep(zc, cot, 0)
        if s == 4:
            loads[3].wait()
        route(s - 1)
        dispatch_rows(s - 1)
    loads[4].wait()
    for s in range(1, 5):
        for copy in c_now:
            copy.wait_recv()
        if s < 4:
            c_now = zstep(zc, cot, s)
        if s == 1:
            up_far = relay(up_own, gu, ucol)
            down_own = own(dw, dn, slice(None))
        dispatch_grads(s - 1)

    for copy in loads[:3]:
        copy.wait()
    for copy in dispatched[: 4 * 7]:
        copy.wait_recv()
    for copy in gate_far + up_far:
        copy.wait_recv()

    def forward_tile(n, carry):
        a = pl.ds(pl.multiple_of(n * 256, 256), 256)
        b = pl.ds(pl.multiple_of(n * 256 + FF, 256), 256)
        gate_pre = dot(rows[...], gu[:, a])
        gp[:, a] = gate_pre
        up_pre = dot(rows[...], gu[:, b])
        gp[:, b] = up_pre
        hid[:, a] = (gate_pre * (1.0 / (1.0 + jnp.exp(-gate_pre))) * up_pre).astype(BF)
        return carry

    lax.fori_loop(0, FF // 256, forward_tile, 0)
    for copy in dispatched[4 * 7 :]:
        copy.wait_recv()

    def term(src, rhs, dy, store):
        def tile(i, carry):
            cols = pl.ds(pl.multiple_of(((y + dy + NY) % NY) * DY + i * 256, 256), 256)
            store(pl.ds(pl.multiple_of(i * 256, 256), 256), dot(src[:, cols], rhs[...], TN))
            return carry

        lax.fori_loop(0, DY // 256, tile, 0)

    def into(buf):
        def store(where, value):
            buf[where, :] = value.astype(buf.dtype)

        return store

    def shares(src, rhs, s1, s2, s3, hp, hm, fp, fm, mine):
        term(src, rhs, 2, into(s2))
        half_p = send(s2.at[lo, :], hp, yp)
        half_m = send(s2.at[hi, :], hm, ym)
        term(src, rhs, 1, into(s1))
        early = [send(s1.at[hi, :], fp.at[hi, :], yp)]
        term(src, rhs, -1, into(s3))
        early.append(send(s3.at[lo, :], fm.at[lo, :], ym))
        term(src, rhs, 0, mine)
        return half_p, half_m, early

    def pass_on(state, s1, s3, hp, hm, fp, fm, cuts):
        half_p, half_m, early = state
        late = []
        for n, (start, size) in enumerate(cuts):
            cols = pl.ds(start, size)
            if n == 0:
                half_p.wait_recv()

            def add_p(i, carry, cols=cols):
                r = pl.ds(pl.multiple_of(i * 64, 64), 64)
                s1[r, cols] = (s1[r, cols].astype(F32) + hp[r, cols].astype(F32)).astype(BF)
                return carry

            lax.fori_loop(0, HALF // 64, add_p, 0)
            first = send(s1.at[lo, cols], fp.at[lo, cols], yp)
            if n == 0:
                half_m.wait_recv()

            def add_m(i, carry, cols=cols):
                r = pl.ds(pl.multiple_of(i * 64, 64), 64)
                t = pl.ds(pl.multiple_of(i * 64 + HALF, 64), 64)
                s3[t, cols] = (s3[t, cols].astype(F32) + hm[r, cols].astype(F32)).astype(BF)
                return carry

            lax.fori_loop(0, HALF // 64, add_m, 0)
            late.append((first, send(s3.at[hi, cols], fm.at[hi, cols], ym)))
        return early, late

    def finish(sent, cuts, fp, fm, outs):
        early, late = sent
        for copy in early:
            copy.wait_recv()
        for (start, size), pair, (out, at_col) in zip(cuts, late, outs):
            cols, mine = pl.ds(start, size), pl.ds(at_col, size)
            for copy in pair:
                copy.wait_recv()

            def add(i, carry, cols=cols, mine=mine, out=out):
                r = pl.ds(pl.multiple_of(i * 64, 64), 64)
                out[r, mine] = out[r, mine] + fp[r, cols].astype(F32) + fm[r, cols].astype(F32)
                return carry

            lax.fori_loop(0, DY // 64, add, 0)

    def gate_up(where, value):
        og[where, :] = value[:, :FF]
        ou[where, :] = value[:, FF:]

    down_cuts, gu_cuts = ((0, FF),), ((0, FF), (FF, 512), (FF + 512, 256))

    down_far = relay(down_own, dn, slice(None))
    down_state = shares(grads, hid, d1, d2, d3, dhp, dhm, dfp, dfm, into(od))
    for copy in down_far:
        copy.wait_recv()
    for copy in dispatched:
        copy.wait_send()

    def out_tile(n, carry):
        a = pl.ds(pl.multiple_of(n * 256, 256), 256)
        xs_r[:, a] = dot(hid[...], dn[a, :], NT).astype(BF)
        return carry

    lax.fori_loop(0, D // 256, out_tile, 0)
    back_o = {}
    for j in (3, 2, 1, 0):
        back_o[j] = xsend(xs_r, xr_o, j, from_x)
        piece(xr_o, j, 0)[...] = piece(xs_r, j, 0)[...]

    def backward_tile(n, carry):
        a = pl.ds(pl.multiple_of(n * 256, 256), 256)
        b = pl.ds(pl.multiple_of(n * 256 + FF, 256), 256)
        d_hidden = dot(grads[...], dn[:, a])
        gate_pre = gp[:, a]
        q = 1.0 / (1.0 + jnp.exp(-gate_pre))
        dgu[:, a] = (d_hidden * gp[:, b] * q * (1.0 + gate_pre * (1.0 - q))).astype(BF)
        dgu[:, b] = (d_hidden * (gate_pre * q)).astype(BF)
        return carry

    lax.fori_loop(0, FF // 256, backward_tile, 0)
    down_last = pass_on(down_state, d1, d3, dhp, dhm, dfp, dfm, down_cuts)
    gu_state = shares(rows, dgu, g1, g2, g3, ghp, ghm, gfp, gfm, gate_up)

    def d_rows_tile(n, carry):
        a = pl.ds(pl.multiple_of(n * 256, 256), 256)
        xs_g[:, a] = dot(dgu[...], gu[a, :], NT).astype(BF)
        return carry

    lax.fori_loop(0, D // 256, d_rows_tile, 0)
    back_d = {}
    for j in (3, 2, 1, 0):
        back_d[j] = xsend(xs_g, xr_d, j, from_x)
        piece(xr_d, j, 0)[...] = piece(xs_g, j, 0)[...]

    def ring(q, part, zs, zr, acc, prev):
        h = TOK // 2
        if q == 0:
            acc[...] = part[:TOK]
            zs[0, 0, :h] = part[TOK : TOK + h].astype(BF)
            zs[1, 0, :h] = part[TOK + h :].astype(BF)
            return (
                send(zs.at[0, 0, pl.ds(0, h)], zr.at[0, 0, pl.ds(0, h)], zp),
                send(zs.at[1, 0, pl.ds(0, h)], zr.at[1, 0, pl.ds(0, h)], zq),
            )
        p0, p1 = part[:TOK], part[TOK:]
        prev[0].wait_recv()
        if q == 1:
            zs[0, q, :h] = (p1[:h] + zr[0, 0, :h].astype(F32)).astype(BF)
            zs[0, q, h:] = p1[h:].astype(BF)
        else:
            zs[0, q] = (p1 + zr[0, q - 1].astype(F32)).astype(BF)
        first = send(zs.at[0, q], zr.at[0, q], zp)
        prev[1].wait_recv()
        if q == 1:
            zs[1, q, h:] = (p0[h:] + zr[1, 0, :h].astype(F32)).astype(BF)
            zs[1, q, :h] = p0[:h].astype(BF)
        else:
            zs[1, q] = (p0 + zr[1, q - 1].astype(F32)).astype(BF)
        return first, send(zs.at[1, q], zr.at[1, q], zq)

    def ring_small(q, part, prev):
        if q == 0:
            pgs[1, 0] = part
            pgs[0, 0] = part
            return (send(pgs.at[0, 0], pgr.at[0, 0], zp),)
        prev[0].wait_recv()
        pgs[0, q] = part + pgr[0, q - 1]
        first = send(pgs.at[0, q], pgr.at[0, q], zp)
        if q == 1:
            pgs[1, q] = part
        else:
            prev[1].wait_recv()
            pgs[1, q] = part + pgr[1, q - 1]
        return first, send(pgs.at[1, q], pgr.at[1, q], zq)

    ring_o = ring_p = ring_d = None
    for q in range(4):
        j = 3 - q
        for copy in back_o[j]:
            copy.wait_recv()
        returned = group(xr_o, j)[...]
        w = wm[j]
        w_hi = w.astype(BF)
        w_lo = (w - w_hi.astype(F32)).astype(BF)
        part = dot(w_hi, returned, TN) + dot(w_lo, returned, TN)
        ring_o = ring(q, part, zs_o, zr_o, acc_o, ring_o)
        scores = dot(returned, group(zc, j)[...], NT) * pm[j].astype(F32)
        both = joined(j)
        small = [
            jnp.sum(jnp.where(both[i : i + 1, :] == expert, scores, 0.0), axis=0, keepdims=True)
            for i in range(TOPK)
        ]
        small = jnp.concatenate(small + [jnp.zeros((2, GR), F32)], axis=0)
        ring_p = ring_small(q, small, ring_p)
    gu_last = pass_on(gu_state, g1, g3, ghp, ghm, gfp, gfm, gu_cuts)
    for q in range(4):
        j = 3 - q
        for copy in back_d[j]:
            copy.wait_recv()
        part = dot(pm[j], group(xr_d, j)[...], TN)
        ring_d = ring(q, part, zs_d, zr_d, acc_d, ring_d)

    for copy in ring_o + ring_p:
        copy.wait_recv()
    mixed_o[...] = (acc_o[...] + zr_o[0, 3].astype(F32) + zr_o[1, 3].astype(F32)).astype(BF)
    pg_o[...] = pgs[1, 0] + pgr[1, 3] + pltpu.roll(pgr[0, 3], TOK, 1)
    finish(down_last, down_cuts, dfp, dfm, ((od, 0),))
    for copy in ring_d:
        copy.wait_recv()
    tgrad_o[...] = (acc_d[...] + zr_d[0, 3].astype(F32) + zr_d[1, 3].astype(F32)).astype(BF)
    for copy in started:
        if not any(copy is other for other in dispatched + list(gu_late(gu_last))):
            copy.wait_send()
    finish(gu_last, gu_cuts, gfp, gfm, ((og, 0), (ou, 0), (ou, 512)))
    for copy in gu_late(gu_last):
        copy.wait_send()


def gu_late(sent):
    return [copy for pair in sent[1] for copy in pair]


def write_out(mixed, tgrad, pg, g, u, d, mixed_o, tgrad_o, pg_o, og, ou, od, sem):
    pairs = ((g, og), (u, ou), (d, od), (mixed, mixed_o), (tgrad, tgrad_o))
    copies = [pltpu.make_async_copy(src, dst, sem.at[i]) for i, (src, dst) in enumerate(pairs)]
    for copy in copies:
        copy.start()
    pg_o[...] = pg[:TOPK, :TOK]
    for copy in copies:
        copy.wait()


def layer(tokens, expert_ids, gate_probs, cotangent, gate_proj, up_proj, down_proj):
    vmem = pl.BlockSpec(memory_space=pltpu.VMEM)
    anywhere = pl.BlockSpec(memory_space=pl.ANY)
    v = pltpu.VMEM
    block = [v((DY, FF), BF)] * 3 + [v((HALF, FF), BF)] * 2 + [v((DY, FF), BF)] * 2
    wide = [v((DY, 2 * FF), BF)] * 3 + [v((HALF, 2 * FF), BF)] * 2 + [v((DY, 2 * FF), BF)] * 2
    scratch = [
        v((4 * GR, D), BF), v((4 * GR, D), BF), v((4, 2, 16, GR), F32),
        v((ROWS, D), BF), v((ROWS, D), BF), v((ROWS, D), BF), v((ROWS, D), BF),
        v((D, 2 * FF), BF), v((D, FF), BF),
        v((ROWS, 2 * FF), F32), v((ROWS, FF), BF), v((ROWS, 2 * FF), BF),
        v((ROWS, D), BF), v((ROWS, D), BF),
        v((16, GR), F32), v((4, GR, GR), BF), v((4, GR, GR), F32),
        v((2, 4, TOK, D), BF), v((2, 4, TOK, D), BF), v((2, 4, TOK, D), BF), v((2, 4, TOK, D), BF),
        v((2, 4, 8, GR), F32), v((2, 4, 8, GR), F32), v((TOK, D), F32), v((TOK, D), F32),
        *block, *wide,
        v((TOPK, TOK), jnp.int32), v((TOPK, TOK), F32), pltpu.SemaphoreType.REGULAR,
        pltpu.SemaphoreType.DMA((208,)), pltpu.SemaphoreType.DMA((208,)), pltpu.SemaphoreType.DMA((8,)),
    ]
    shapes = [((TOK, D), BF), ((TOK, D), BF), ((8, GR), F32)] + [((DY, FF), F32)] * 3
    held = pl.pallas_call(
        kernel,
        out_shape=tuple(pltpu.VMEM(shape, dtype) for shape, dtype in shapes),
        in_specs=[anywhere] * 7,
        out_specs=(vmem,) * 6,
        scratch_shapes=scratch,
        name="expert_layer",
        compiler_params=pltpu.CompilerParams(
            collective_id=0, has_side_effects=True, vmem_limit_bytes=VMEM_LIMIT
        ),
    )(tokens, cotangent, expert_ids.T, gate_probs.T, gate_proj[0], up_proj[0], down_proj[0])
    shapes[2] = ((TOPK, TOK), F32)
    mixed, token_grads, prob_grads, grad_gate, grad_up, grad_down = pl.pallas_call(
        write_out,
        out_shape=tuple(jax.ShapeDtypeStruct(shape, dtype) for shape, dtype in shapes),
        in_specs=[vmem] * 6,
        out_specs=(anywhere, anywhere, vmem, anywhere, anywhere, anywhere),
        scratch_shapes=[pltpu.SemaphoreType.DMA((5,))],
        name="write_out",
        compiler_params=pltpu.CompilerParams(vmem_limit_bytes=1024 * 1024),
    )(*(pltpu.with_memory_space_constraint(part, pltpu.VMEM) for part in held))
    return (
        mixed, token_grads, prob_grads.T, grad_gate[None], grad_up[None], grad_down[None],
    )


def solution(mesh):
    rows, weights = P(("dp", "expert"), None), P("expert", "dp", None)
    return jax.shard_map(
        layer,
        mesh=mesh,
        in_specs=(rows,) * 4 + (weights,) * 3,
        out_specs=(rows,) * 3 + (weights,) * 3,
        check_vma=False,
    )
```

```python
import jax
import jax.numpy as jnp
from jax import lax
from jax.experimental import pallas as pl
from jax.experimental.pallas import tpu as pltpu
from jax.sharding import PartitionSpec as P

MESH = pl.DeviceIdType.MESH
BF = jnp.bfloat16
F32 = jnp.float32
NY, NZ, NX, NC = 4, 8, 4, 2
TOK, D, FF, CAP, TOPK = 64, 2048, 768, 8, 6
ROWS = NX * NC * NZ * CAP
GR = 2 * TOK
DY = D // NY
HALF = DY // 2
NT = (((1,), (1,)), ((), ()))
TN = (((0,), (0,)), ((), ()))
VMEM_LIMIT = 57 * 1024 * 1024


def dot(a, b, dims=(((1,), (0,)), ((), ()))):
    return lax.dot_general(a, b, dims, preferred_element_type=F32)


def kernel(
    tok, cot, ids, probs, gw, uw, dw,
    mixed_o, tgrad_o, pg_o, og, ou, od,
    zt, zc, zm, xs_r, xs_g, rows, grads, gu, dn, gp, hid, dgu, xr_o, xr_d,
    meta, pm, wm, zs_o, zr_o, zs_d, zr_d, pgs, pgr, acc_o, acc_d,
    d1, d2, d3, dhp, dhm, dfp, dfm,
    g1, g2, g3, ghp, ghm, gfp, gfm,
    ids_v, probs_v, go, ssem, rsem, lsem,
):
    y = lax.axis_index("dp")
    e = lax.axis_index("expert")
    z, x, c = e // (NX * NC), (e // NC) % NX, e % NC

    def at(dy=0, dz=0, dx=0, dc=0):
        return (
            (y + dy + NY) % NY,
            ((z + dz + NZ) % NZ) * (NX * NC) + ((x + dx + NX) % NX) * NC + (c + dc) % NC,
        )

    yp, ym, zp, zq = at(dy=1), at(dy=-1), at(dz=1), at(dz=-1)
    offsets = [(k // NC, k % NC) for k in range(NX * NC)]
    to_x = [at(dx=dx, dc=dc) for dx, dc in offsets]
    from_x = [at(dx=-dx, dc=dc) for dx, dc in offsets]

    barrier = pltpu.get_barrier_semaphore()

    def tell(peer):
        pl.semaphore_signal(barrier, inc=1, device_id=peer, device_id_type=MESH)

    other, first, second = at(dc=1), (NC - c) % NC, 1 - c
    for dy in (1, -1):
        tell(at(dy=dy, dc=first))
    for dz in (1, -1):
        tell(at(dz=dz, dc=second))
    for dx in range(1, NX):
        tell(at(dx=dx, dc=second))
    tell(other)

    @pl.when(c == 0)
    def _():
        pl.semaphore_wait(barrier, NC * 2 + 1)
        pl.semaphore_signal(go, inc=1, device_id=other, device_id_type=MESH)

    @pl.when(c == 1)
    def _():
        pl.semaphore_wait(go, 1)

    used = [0, 0]
    started = []

    def send(src, dst, peer):
        i = used[0]
        used[0] += 1
        copy = pltpu.make_async_remote_copy(
            src_ref=src, dst_ref=dst, send_sem=ssem.at[i], recv_sem=rsem.at[i],
            device_id=peer, device_id_type=MESH,
        )
        copy.start()
        started.append(copy)
        return copy

    def local(src, dst):
        i = used[1]
        used[1] += 1
        copy = pltpu.make_async_copy(src, dst, lsem.at[i])
        copy.start()
        return copy

    def yrows(dy, start=0, size=DY):
        return pl.ds(pl.multiple_of(((y + dy + NY) % NY) * DY + start, HALF), size)

    gcol, ucol = pl.ds(0, FF), pl.ds(FF, FF)

    lo, hi = pl.ds(0, HALF), pl.ds(HALF, HALF)

    def own(w, full, cols):
        first, second = full.at[yrows(0, 0, HALF), cols], full.at[yrows(0, HALF, HALF), cols]
        return (
            send(w.at[lo, :], first, yp),
            send(w.at[hi, :], second, ym),
            send(w.at[hi, :], second, yp),
            send(w.at[lo, :], first, ym),
        )

    def relay(parts, full, cols):
        parts[0].wait_recv()
        a = full.at[yrows(-1, 0, HALF), cols]
        first = send(a, a, yp)
        parts[1].wait_recv()
        b = full.at[yrows(1, HALF, HALF), cols]
        return first, send(b, b, ym), parts[2], parts[3]

    gate_own = own(gw, gu, gcol)
    up_own = own(uw, gu, ucol)
    tables = [local(ids, ids_v), local(probs, probs_v)]

    def zblock(buf, j, zi, start=0, size=TOK):
        return buf.at[pl.ds(j * GR + zi * TOK + start, size), :]

    def zstep(buf, src, s):
        if s == 0:
            return send(src, zblock(buf, 0, 0), zp), send(src, zblock(buf, 0, 1), zq)
        if s < 3:
            return (
                send(zblock(buf, s - 1, 0), zblock(buf, s, 0), zp),
                send(zblock(buf, s - 1, 1), zblock(buf, s, 1), zq),
            )
        h = TOK // 2
        return (
            send(zblock(buf, 2, 0, 0, h), zblock(buf, 3, 1, 0, h), zp),
            send(zblock(buf, 2, 1, h, h), zblock(buf, 3, 1, h, h), zq),
        )

    def mstep(s):
        if s == 0:
            return send(meta, zm.at[0, 0], zp), send(meta, zm.at[0, 1], zq)
        if s < 3:
            return send(zm.at[s - 1, 0], zm.at[s, 0], zp), send(zm.at[s - 1, 1], zm.at[s, 1], zq)
        return (send(zm.at[2, 0], zm.at[3, 1], zp),)

    for copy in tables:
        copy.wait()
    meta[...] = jnp.full(meta.shape, -1.0, F32)
    for start in (0, TOK):
        meta[0:TOPK, start : start + TOK] = ids_v[...].astype(F32)
        meta[8 : 8 + TOPK, start : start + TOK] = probs_v[...]

    @pl.when(c == 1)
    def _():
        pl.semaphore_wait(barrier, 1 + NC * 2 + NC * (NX - 1))
        pl.semaphore_signal(go, inc=1, device_id=other, device_id_type=MESH)

    @pl.when(c == 0)
    def _():
        pl.semaphore_wait(go, 1)

    m_now = mstep(0)
    t_now = zstep(zt, tok, 0)
    loads = [
        local(gw, gu.at[yrows(0), gcol]),
        local(uw, gu.at[yrows(0), ucol]),
        local(dw, dn.at[yrows(0), :]),
        local(tok, zblock(zt, 3, 0)),
        local(cot, zblock(zc, 3, 0)),
    ]
    zm[3, 0] = meta[...]

    row = lax.broadcasted_iota(jnp.int32, (GR, GR), 0)
    lane = lax.broadcasted_iota(jnp.int32, (GR, GR), 1)
    kk = row >> 4
    expert = (z * (NX * NC) + (((x + (kk >> 1)) & (NX - 1)) << 1) + ((c + kk) & 1)).astype(F32)
    slot = (row & (CAP - 1)).astype(F32)
    same_block = ((row >> 3) & 1) == (lane >> 6)
    earlier = jnp.where(((row >> 6) == (lane >> 6)) & (row < lane), 1.0, 0.0).astype(BF)
    low = lax.broadcasted_iota(jnp.int32, (16, GR), 1) < TOK

    def joined(j):
        return jnp.where(low, zm[j, 0], zm[j, 1])

    def route(j):
        both = joined(j)
        named = jnp.zeros((GR, GR), F32)
        weight = jnp.zeros((GR, GR), F32)
        for i in range(TOPK):
            hit = both[i : i + 1, :] == expert
            named = jnp.where(hit, 1.0, named)
            weight = weight + jnp.where(hit, both[8 + i : 9 + i, :], 0.0)
        rank = dot(named.astype(BF), earlier)
        fits = (named > 0.5) & (rank == slot) & same_block
        pm[j] = jnp.where(fits, 1.0, 0.0).astype(BF)
        wm[j] = jnp.where(fits, weight, 0.0)

    def group(buf, j):
        return buf.at[pl.ds(j * GR, GR), :]

    def piece(buf, j, k):
        return buf.at[pl.ds(j * GR + k * 16, 16), :]

    def xsend(src, dst, j, targets):
        return [send(piece(src, j, k), piece(dst, j, k), targets[k]) for k in range(1, NX * NC)]

    dispatched = []

    def dispatch_rows(j):
        filled = dot(pm[j], group(zt, j)[...]).astype(BF)
        group(xs_r, j)[...] = filled
        piece(rows, j, 0)[...] = filled[:16]
        dispatched.extend(xsend(xs_r, rows, j, to_x))

    def dispatch_grads(j):
        prob = jnp.sum(wm[j], axis=1, keepdims=True)
        filled = (dot(pm[j], group(zc, j)[...]) * prob).astype(BF)
        group(xs_g, j)[...] = filled
        piece(grads, j, 0)[...] = filled[:16]
        dispatched.extend(xsend(xs_g, grads, j, to_x))

    c_now = None
    gate_far = up_far = down_own = None
    for s in range(1, 5):
        t_next = m_next = None
        for copy in m_now:
            copy.wait_recv()
        if s < 4:
            m_now = mstep(s)
        for copy in t_now:
            copy.wait_recv()
        if s < 4:
            t_now = zstep(zt, tok, s)
        if s == 2:
            gate_far = relay(gate_own, gu, gcol)
        if s == 3:
            c_now = zstep(zc, cot, 0)
        if s == 4:
            loads[3].wait()
        route(s - 1)
        dispatch_rows(s - 1)
    loads[4].wait()
    for s in range(1, 5):
        for copy in c_now:
            copy.wait_recv()
        if s < 4:
            c_now = zstep(zc, cot, s)
        if s == 1:
            up_far = relay(up_own, gu, ucol)
            down_own = own(dw, dn, slice(None))
        dispatch_grads(s - 1)

    for copy in loads[:3]:
        copy.wait()
    for copy in dispatched[: 4 * 7]:
        copy.wait_recv()
    for copy in gate_far + up_far:
        copy.wait_recv()

    def forward_tile(n, carry):
        a = pl.ds(pl.multiple_of(n * 256, 256), 256)
        b = pl.ds(pl.multiple_of(n * 256 + FF, 256), 256)
        gate_pre = dot(rows[...], gu[:, a])
        gp[:, a] = gate_pre
        up_pre = dot(rows[...], gu[:, b])
        gp[:, b] = up_pre
        hid[:, a] = (gate_pre * (1.0 / (1.0 + jnp.exp(-gate_pre))) * up_pre).astype(BF)
        return carry

    lax.fori_loop(0, FF // 256, forward_tile, 0)
    for copy in dispatched[4 * 7 :]:
        copy.wait_recv()

    def term(src, rhs, dy, store):
        def tile(i, carry):
            cols = pl.ds(pl.multiple_of(((y + dy + NY) % NY) * DY + i * 256, 256), 256)
            store(pl.ds(pl.multiple_of(i * 256, 256), 256), dot(src[:, cols], rhs[...], TN))
            return carry

        lax.fori_loop(0, DY // 256, tile, 0)

    def into(buf):
        def store(where, value):
            buf[where, :] = value.astype(buf.dtype)

        return store

    def shares(src, rhs, s1, s2, s3, hp, hm, fp, fm, mine):
        term(src, rhs, 2, into(s2))
        half_p = send(s2.at[lo, :], hp, yp)
        half_m = send(s2.at[hi, :], hm, ym)
        term(src, rhs, 1, into(s1))
        early = [send(s1.at[hi, :], fp.at[hi, :], yp)]
        term(src, rhs, -1, into(s3))
        early.append(send(s3.at[lo, :], fm.at[lo, :], ym))
        term(src, rhs, 0, mine)
        return half_p, half_m, early

    def pass_on(state, s1, s3, hp, hm, fp, fm, cuts):
        half_p, half_m, early = state
        late = []
        for n, (start, size) in enumerate(cuts):
            cols = pl.ds(start, size)
            if n == 0:
                half_p.wait_recv()

            def add_p(i, carry, cols=cols):
                r = pl.ds(pl.multiple_of(i * 64, 64), 64)
                s1[r, cols] = (s1[r, cols].astype(F32) + hp[r, cols].astype(F32)).astype(BF)
                return carry

            lax.fori_loop(0, HALF // 64, add_p, 0)
            first = send(s1.at[lo, cols], fp.at[lo, cols], yp)
            if n == 0:
                half_m.wait_recv()

            def add_m(i, carry, cols=cols):
                r = pl.ds(pl.multiple_of(i * 64, 64), 64)
                t = pl.ds(pl.multiple_of(i * 64 + HALF, 64), 64)
                s3[t, cols] = (s3[t, cols].astype(F32) + hm[r, cols].astype(F32)).astype(BF)
                return carry

            lax.fori_loop(0, HALF // 64, add_m, 0)
            late.append((first, send(s3.at[hi, cols], fm.at[hi, cols], ym)))
        return early, late

    def finish(sent, cuts, fp, fm, outs):
        early, late = sent
        for copy in early:
            copy.wait_recv()
        for (start, size), pair, (out, at_col) in zip(cuts, late, outs):
            cols, mine = pl.ds(start, size), pl.ds(at_col, size)
            for copy in pair:
                copy.wait_recv()

            def add(i, carry, cols=cols, mine=mine, out=out):
                r = pl.ds(pl.multiple_of(i * 64, 64), 64)
                out[r, mine] = out[r, mine] + fp[r, cols].astype(F32) + fm[r, cols].astype(F32)
                return carry

            lax.fori_loop(0, DY // 64, add, 0)

    def gate_up(where, value):
        og[where, :] = value[:, :FF]
        ou[where, :] = value[:, FF:]

    down_cuts, gu_cuts = ((0, FF),), ((0, FF), (FF, 512), (FF + 512, 256))

    down_far = relay(down_own, dn, slice(None))
    down_state = shares(grads, hid, d1, d2, d3, dhp, dhm, dfp, dfm, into(od))
    for copy in down_far:
        copy.wait_recv()
    for copy in dispatched:
        copy.wait_send()

    def out_tile(n, carry):
        a = pl.ds(pl.multiple_of(n * 256, 256), 256)
        xs_r[:, a] = dot(hid[...], dn[a, :], NT).astype(BF)
        return carry

    lax.fori_loop(0, D // 256, out_tile, 0)
    back_o = {}
    for j in (3, 2, 1, 0):
        back_o[j] = xsend(xs_r, xr_o, j, from_x)
        piece(xr_o, j, 0)[...] = piece(xs_r, j, 0)[...]

    def backward_tile(n, carry):
        a = pl.ds(pl.multiple_of(n * 256, 256), 256)
        b = pl.ds(pl.multiple_of(n * 256 + FF, 256), 256)
        d_hidden = dot(grads[...], dn[:, a])
        gate_pre = gp[:, a]
        q = 1.0 / (1.0 + jnp.exp(-gate_pre))
        dgu[:, a] = (d_hidden * gp[:, b] * q * (1.0 + gate_pre * (1.0 - q))).astype(BF)
        dgu[:, b] = (d_hidden * (gate_pre * q)).astype(BF)
        return carry

    lax.fori_loop(0, FF // 256, backward_tile, 0)
    down_last = pass_on(down_state, d1, d3, dhp, dhm, dfp, dfm, down_cuts)
    gu_state = shares(rows, dgu, g1, g2, g3, ghp, ghm, gfp, gfm, gate_up)

    def d_rows_tile(n, carry):
        a = pl.ds(pl.multiple_of(n * 256, 256), 256)
        xs_g[:, a] = dot(dgu[...], gu[a, :], NT).astype(BF)
        return carry

    lax.fori_loop(0, D // 256, d_rows_tile, 0)
    back_d = {}
    for j in (3, 2, 1, 0):
        back_d[j] = xsend(xs_g, xr_d, j, from_x)
        piece(xr_d, j, 0)[...] = piece(xs_g, j, 0)[...]

    def ring(q, part, zs, zr, acc, prev):
        h = TOK // 2
        if q == 0:
            acc[...] = part[:TOK]
            zs[0, 0, :h] = part[TOK : TOK + h].astype(BF)
            zs[1, 0, :h] = part[TOK + h :].astype(BF)
            return (
                send(zs.at[0, 0, pl.ds(0, h)], zr.at[0, 0, pl.ds(0, h)], zp),
                send(zs.at[1, 0, pl.ds(0, h)], zr.at[1, 0, pl.ds(0, h)], zq),
            )
        p0, p1 = part[:TOK], part[TOK:]
        prev[0].wait_recv()
        if q == 1:
            zs[0, q, :h] = (p1[:h] + zr[0, 0, :h].astype(F32)).astype(BF)
            zs[0, q, h:] = p1[h:].astype(BF)
        else:
            zs[0, q] = (p1 + zr[0, q - 1].astype(F32)).astype(BF)
        first = send(zs.at[0, q], zr.at[0, q], zp)
        prev[1].wait_recv()
        if q == 1:
            zs[1, q, h:] = (p0[h:] + zr[1, 0, :h].astype(F32)).astype(BF)
            zs[1, q, :h] = p0[:h].astype(BF)
        else:
            zs[1, q] = (p0 + zr[1, q - 1].astype(F32)).astype(BF)
        return first, send(zs.at[1, q], zr.at[1, q], zq)

    def ring_small(q, part, prev):
        if q == 0:
            pgs[1, 0] = part
            pgs[0, 0] = part
            return (send(pgs.at[0, 0], pgr.at[0, 0], zp),)
        prev[0].wait_recv()
        pgs[0, q] = part + pgr[0, q - 1]
        first = send(pgs.at[0, q], pgr.at[0, q], zp)
        if q == 1:
            pgs[1, q] = part
        else:
            prev[1].wait_recv()
            pgs[1, q] = part + pgr[1, q - 1]
        return first, send(pgs.at[1, q], pgr.at[1, q], zq)

    ring_o = ring_p = ring_d = None
    for q in range(4):
        j = 3 - q
        for copy in back_o[j]:
            copy.wait_recv()
        returned = group(xr_o, j)[...]
        w = wm[j]
        w_hi = w.astype(BF)
        w_lo = (w - w_hi.astype(F32)).astype(BF)
        part = dot(w_hi, returned, TN) + dot(w_lo, returned, TN)
        ring_o = ring(q, part, zs_o, zr_o, acc_o, ring_o)
        scores = dot(returned, group(zc, j)[...], NT) * pm[j].astype(F32)
        both = joined(j)
        small = [
            jnp.sum(jnp.where(both[i : i + 1, :] == expert, scores, 0.0), axis=0, keepdims=True)
            for i in range(TOPK)
        ]
        small = jnp.concatenate(small + [jnp.zeros((2, GR), F32)], axis=0)
        ring_p = ring_small(q, small, ring_p)
    gu_last = pass_on(gu_state, g1, g3, ghp, ghm, gfp, gfm, gu_cuts)
    for q in range(4):
        j = 3 - q
        for copy in back_d[j]:
            copy.wait_recv()
        part = dot(pm[j], group(xr_d, j)[...], TN)
        ring_d = ring(q, part, zs_d, zr_d, acc_d, ring_d)

    for copy in ring_o + ring_p:
        copy.wait_recv()
    mixed_o[...] = (acc_o[...] + zr_o[0, 3].astype(F32) + zr_o[1, 3].astype(F32)).astype(BF)
    pg_o[...] = pgs[1, 0] + pgr[1, 3] + pltpu.roll(pgr[0, 3], TOK, 1)
    finish(down_last, down_cuts, dfp, dfm, ((od, 0),))
    for copy in ring_d:
        copy.wait_recv()
    tgrad_o[...] = (acc_d[...] + zr_d[0, 3].astype(F32) + zr_d[1, 3].astype(F32)).astype(BF)
    for copy in started:
        if not any(copy is other for other in dispatched + list(gu_late(gu_last))):
            copy.wait_send()
    finish(gu_last, gu_cuts, gfp, gfm, ((og, 0), (ou, 0), (ou, 512)))
    for copy in gu_late(gu_last):
        copy.wait_send()


def gu_late(sent):
    return [copy for pair in sent[1] for copy in pair]


def write_out(mixed, tgrad, pg, g, u, d, mixed_o, tgrad_o, pg_o, og, ou, od, sem):
    pairs = ((g, og), (u, ou), (d, od), (mixed, mixed_o), (tgrad, tgrad_o))
    copies = [pltpu.make_async_copy(src, dst, sem.at[i]) for i, (src, dst) in enumerate(pairs)]
    for copy in copies:
        copy.start()
    pg_o[...] = pg[:TOPK, :TOK]
    for copy in copies:
        copy.wait()


def layer(tokens, expert_ids, gate_probs, cotangent, gate_proj, up_proj, down_proj):
    vmem = pl.BlockSpec(memory_space=pltpu.VMEM)
    anywhere = pl.BlockSpec(memory_space=pl.ANY)
    v = pltpu.VMEM
    block = [v((DY, FF), BF)] * 3 + [v((HALF, FF), BF)] * 2 + [v((DY, FF), BF)] * 2
    wide = [v((DY, 2 * FF), BF)] * 3 + [v((HALF, 2 * FF), BF)] * 2 + [v((DY, 2 * FF), BF)] * 2
    scratch = [
        v((4 * GR, D), BF), v((4 * GR, D), BF), v((4, 2, 16, GR), F32),
        v((ROWS, D), BF), v((ROWS, D), BF), v((ROWS, D), BF), v((ROWS, D), BF),
        v((D, 2 * FF), BF), v((D, FF), BF),
        v((ROWS, 2 * FF), F32), v((ROWS, FF), BF), v((ROWS, 2 * FF), BF),
        v((ROWS, D), BF), v((ROWS, D), BF),
        v((16, GR), F32), v((4, GR, GR), BF), v((4, GR, GR), F32),
        v((2, 4, TOK, D), BF), v((2, 4, TOK, D), BF), v((2, 4, TOK, D), BF), v((2, 4, TOK, D), BF),
        v((2, 4, 8, GR), F32), v((2, 4, 8, GR), F32), v((TOK, D), F32), v((TOK, D), F32),
        *block, *wide,
        v((TOPK, TOK), jnp.int32), v((TOPK, TOK), F32), pltpu.SemaphoreType.REGULAR,
        pltpu.SemaphoreType.DMA((208,)), pltpu.SemaphoreType.DMA((208,)), pltpu.SemaphoreType.DMA((8,)),
    ]
    shapes = [((TOK, D), BF), ((TOK, D), BF), ((8, GR), F32)] + [((DY, FF), F32)] * 3
    held = pl.pallas_call(
        kernel,
        out_shape=tuple(pltpu.VMEM(shape, dtype) for shape, dtype in shapes),
        in_specs=[anywhere] * 7,
        out_specs=(vmem,) * 6,
        scratch_shapes=scratch,
        name="expert_layer",
        compiler_params=pltpu.CompilerParams(
            collective_id=0, has_side_effects=True, vmem_limit_bytes=VMEM_LIMIT
        ),
    )(tokens, cotangent, expert_ids.T, gate_probs.T, gate_proj[0], up_proj[0], down_proj[0])
    shapes[2] = ((TOPK, TOK), F32)
    mixed, token_grads, prob_grads, grad_gate, grad_up, grad_down = pl.pallas_call(
        write_out,
        out_shape=tuple(jax.ShapeDtypeStruct(shape, dtype) for shape, dtype in shapes),
        in_specs=[vmem] * 6,
        out_specs=(anywhere, anywhere, vmem, anywhere, anywhere, anywhere),
        scratch_shapes=[pltpu.SemaphoreType.DMA((5,))],
        name="write_out",
        compiler_params=pltpu.CompilerParams(vmem_limit_bytes=1024 * 1024),
    )(*(pltpu.with_memory_space_constraint(part, pltpu.VMEM) for part in held))
    return (
        mixed, token_grads, prob_grads.T, grad_gate[None], grad_up[None], grad_down[None],
    )


def solution(mesh):
    rows, weights = P(("dp", "expert"), None), P("expert", "dp", None)
    return jax.shard_map(
        layer,
        mesh=mesh,
        in_specs=(rows,) * 4 + (weights,) * 3,
        out_specs=(rows,) * 3 + (weights,) * 3,
        check_vma=False,
    )
```
